32 devices in a mesh: mem: 8 (over z, y), job: 4 (over x, core).
Axes of the slice: x: 2, y: 2, z: 4, core: 2. Of those that a mesh axis runs over, the one named last changes fastest.
Arguments:
- pair_cost: bfloat16 [1536, 128, 128], P(('mem', 'job')), may hold values from -6 to 6
- pair_coef: bfloat16 [1536, 128, 128], P(('mem', 'job')), may hold values from 0.049804688 to 0.5
- slot_member: int32 [32, 48], P(('mem', 'job')), may hold values from 0 to 31, never falling along the last dimension, each value on 1 to 4 neighbouring positions
- slot_owner: int32 [32, 48, 1], P(('mem', 'job')), may hold values from 0 to 7; in each aligned block of 48 rows (0 to 47, 48 to 95, ..., all dimensions but the last counted through in order) at most 9 rows name the same one
- slot_local: int32 [32, 48], P(('mem', 'job')), may hold values from 0 to 15
- duals: float32 [512, 128], P(('mem', 'job')), may hold values from 0.1 to 3
- capacity: int32 [512, 128], P(('mem', 'job')), may hold values from 0 to 39
Outputs:
- primal: bfloat16 [1536, 128, 128], P(('mem', 'job'))
- gradient: float32 [512, 128], P(('mem', 'job'))
- member_share: float32 [256, 128], P('mem')
The draws below stay inside these ranges and needn't reach their ends.
Inputs may be any that keep to these rules, and one draw needn't show every extreme that they name: `slot_member`: in each device's row the values never fall, every value appears, none more than 4 times, and one exactly 4 times. `slot_owner`: among the 48 entries of one device no value appears more than 9 times, and in some devices one appears exactly 9 times.
All inputs are finite; a program needn't handle non-finite values.
Results may differ from the reference program's by a relative error of at most 0.001.
Values sent between devices are 32-bit elements; how exact they have to be, the bound alone decides.
A program may use at most 64 MiB of HBM per device.

```python
import math
import jax
import jax.numpy as jnp
import numpy as np
from jax import lax

BLOCK = 128
CAP = 48
MB_DEV = 32
JB_DEV = 16
SEG_MOST = 4
PEER_MOST = 9
NBLK = 1536
MBLK = 256
JBLK = 512
N_MEM = 8
N_JOB = 4


def plant(array, key, least, high):
    place = [jax.random.randint(jax.random.fold_in(key, axis), (), 0, length) for axis, length in enumerate(array.shape)]
    longest = array.shape.index(max(array.shape))
    neighbour = place[:longest] + [(place[longest] + 1) % array.shape[longest]] + place[longest + 1:]
    return array.at[tuple(place)].set(least).at[tuple(neighbour)].set(high)


def shard_levels(key, shape, pieces, least, high):
    def one(position, blocks):
        draws = jax.random.uniform(jax.random.fold_in(jax.random.fold_in(key, 6), position), (blocks,), jnp.float32, least / len(pieces), high / len(pieces))
        return jnp.repeat(jnp.exp(draws), shape[position] // blocks).reshape((-1,) + (1,) * (len(shape) - position - 1))

    factor_of = one(*pieces[0])
    for cut in pieces[1:]:
        factor_of = factor_of * one(*cut)
    return factor_of


def split_up(number_of, total, reach, lean):
    portions = [(1 << 20) // math.isqrt(grade ** lean) + 1 for grade in range(2, number_of + 1)]
    rest, counts = total - reach - (number_of - 1), [1] * (number_of - 1)
    while rest > 0:
        candidates = [i for i in range(number_of - 1) if counts[i] < reach]
        mass, left = sum([portions[i] for i in candidates]), rest
        for i in candidates:
            more = min(reach - counts[i], max(1, left * portions[i] // mass), rest)
            counts[i] = counts[i] + more
            rest = rest - more
    return np.array([reach] + counts)


def uneven(rng, amount, total, limit, slope):
    if amount == 2:
        one = jax.random.randint(rng, (), max(1, total - limit), min(limit, total - 1) + 1)
        return jnp.stack([one, total - one])
    sizes = jnp.asarray(split_up(amount, total, limit, slope), jnp.int32)
    couples = (amount - 1) // 2
    source_of, receiver = sizes[1:1 + 2 * couples:2], sizes[2:2 + 2 * couples:2]
    slack = jnp.minimum(source_of - 1, limit - receiver)
    passed = jax.random.randint(jax.random.fold_in(rng, 1), (couples,), 0, 1 << 20) % (slack + 1)
    sizes = sizes.at[1:1 + 2 * couples:2].set(source_of - passed).at[2:2 + 2 * couples:2].set(receiver + passed)
    return sizes[jax.random.permutation(jax.random.fold_in(rng, 2), amount)]


def shared_out(own_key, own, number, rows, amount, top, limit, skew):
    ranking = jax.random.permutation(own_key, amount)
    crowded, ordinary = shares(amount, rows * top, limit, skew, True), shares(amount, rows * top, limit, skew, False)
    places = jnp.arange(amount)

    def named(sizes, offset_by):
        used = int((sizes > 0).sum())
        fixed = max(1, used // 4)
        moved = fixed + (places - fixed + offset_by * (used - fixed)) % max(1, amount - fixed)
        return jnp.zeros((amount,), jnp.int32).at[ranking[jnp.where(places < fixed, places, moved)]].set(jnp.asarray(sizes, jnp.int32))

    sizes = jnp.where(number % 4 == 0, named(crowded, number // 4), named(ordinary, number - number // 4 - 1))
    mixed = jax.random.permutation(jax.random.fold_in(own, 3), amount)
    giver, receiver = mixed[0:amount // 2 * 2:2], mixed[1:amount // 2 * 2:2]
    room = jnp.minimum(sizes[giver] - 1, limit - sizes[receiver]) // 2
    room = jnp.where((giver == ranking[0]) | (receiver == ranking[0]) | (sizes[receiver] == 0), 0, jnp.maximum(room, 0))
    moved = jax.random.randint(jax.random.fold_in(own, 4), (amount // 2,), 0, 1 << 20) % (room + 1)
    sizes = sizes.at[giver].add(-moved).at[receiver].add(moved)
    items = jnp.searchsorted(jnp.cumsum(sizes), jnp.arange(rows * top), side="right").astype(jnp.int32)
    grid = items.reshape(top, rows).T
    grid = grid[jax.random.permutation(jax.random.fold_in(own, 1), rows)]
    offset_by = jax.random.randint(jax.random.fold_in(own, 2), (rows, 1), 0, top)
    return jnp.take_along_axis(grid, (jnp.arange(top)[None, :] + offset_by) % top, axis=1)


def shares(number_of, total, reach, skew, full):
    weights = [(1 << 20) // math.isqrt(standing ** skew) + 1 for standing in range(1, number_of + 1)]
    largest = reach if full else min(reach, max(-(-total // number_of), total * weights[0] // sum(weights)))
    least = 1 if total - largest >= number_of - 1 else 0
    holding, rest = [largest] + [least] * (number_of - 1), total - largest - least * (number_of - 1)
    while rest > 0:
        candidates = [i for i in range(1, number_of) if holding[i] < largest] or [i for i in range(1, number_of) if holding[i] < reach]
        mass, budget = sum([weights[i] for i in candidates]), rest
        for i in candidates:
            addition = min(reach - holding[i], max(1, budget * weights[i] // mass), rest)
            holding[i] = holding[i] + addition
            rest = rest - addition
    return np.array(holding)


def gaussian(key, extent, width, bound, shards=(), kind=jnp.bfloat16):
    level = shard_levels(key, extent, shards, -0.22, 0.18) if shards else 1.0
    array = jax.random.normal(key, extent, jnp.float32) * width * level
    return jnp.minimum(jnp.maximum(array, -bound), bound).astype(kind)


def setup_inputs(seed: int = 0) -> dict:
    keys = jax.random.split(jax.random.key(seed), 8)
    pair_cost = gaussian(keys[0], (NBLK, BLOCK, BLOCK), 1.0, 6.0, ((0, 32),))
    pair_coef = jnp.clip(jnp.exp(math.log(0.5) - 2.306499 * jax.random.uniform(keys[1], (NBLK, BLOCK, BLOCK), jnp.float32) ** shard_levels(keys[1], (NBLK, BLOCK, BLOCK), ((0, 32),), -0.2, 0.2)), 0.049804688, 0.5).astype(jnp.bfloat16)
    slot_member = jax.vmap(lambda own: jnp.searchsorted(jnp.cumsum(uneven(own, MB_DEV, CAP, SEG_MOST, 2)), jnp.arange(CAP), side="right"))(jax.random.split(keys[2], (N_MEM * N_JOB))).reshape((N_MEM * N_JOB, CAP)).astype(jnp.int32)
    slot_owner_keys = jax.random.split(jax.random.fold_in(keys[3], 1), (N_MEM * N_JOB) * CAP // CAP)
    slot_owner_turns = jax.random.permutation(jax.random.fold_in(keys[3], 3), (N_MEM * N_JOB) * CAP // CAP)
    slot_owner = jax.vmap(lambda own, number: shared_out(jax.random.fold_in(keys[3], 2), own, number, CAP, N_MEM, 1, PEER_MOST, 2))(slot_owner_keys, slot_owner_turns).reshape((N_MEM * N_JOB, CAP, 1))
    slot_local = plant(jax.random.randint(keys[4], (N_MEM * N_JOB, CAP), 0, JB_DEV), jax.random.fold_in(keys[4], 1), 0, JB_DEV - 1).astype(jnp.int32)
    duals = jnp.clip(jnp.exp(math.log(3.0) - 3.4011974 * jax.random.uniform(keys[5], (JBLK, BLOCK), jnp.float32) ** shard_levels(keys[5], (JBLK, BLOCK), ((0, 32),), -0.2, 0.2)), 0.1, 3.0)
    capacity = plant(jax.random.randint(keys[6], (JBLK, BLOCK), 0, 40), jax.random.fold_in(keys[6], 1), 0, 39).astype(jnp.int32)
    return dict(pair_cost=pair_cost, pair_coef=pair_coef, slot_member=slot_member, slot_owner=slot_owner, slot_local=slot_local, duals=duals, capacity=capacity)


RIDGE = 1.0


def slot_terms(packed):
    pair_cost, pair_coef, dual_rows = packed
    reduced = pair_cost.astype(jnp.float32) + pair_coef.astype(jnp.float32) * dual_rows[:, None, :]
    allocation = jnp.clip(-reduced / RIDGE, 0.0, 1.0)
    column_part = jnp.sum(pair_coef.astype(jnp.float32) * allocation, axis=1)
    row_part = jnp.sum(allocation, axis=2)
    return allocation.astype(jnp.bfloat16), column_part, row_part


def reference(pair_cost, pair_coef, slot_member, slot_owner, slot_local, duals, capacity):
    device = jnp.arange(N_MEM * N_JOB, dtype=jnp.int32)
    column = device % N_JOB
    job_block = (slot_owner[:, :, 0] * N_JOB + column[:, None]) * JB_DEV + slot_local
    member_block = (device // N_JOB)[:, None] * MB_DEV + slot_member
    dual_rows = duals[job_block.reshape(-1)].reshape(N_MEM * N_JOB, CAP, BLOCK)
    cost_dev = pair_cost.reshape(N_MEM * N_JOB, CAP, BLOCK, BLOCK)
    coef_dev = pair_coef.reshape(N_MEM * N_JOB, CAP, BLOCK, BLOCK)
    primal, column_part, row_part = lax.map(slot_terms, (cost_dev, coef_dev, dual_rows))
    totals = jax.ops.segment_sum(column_part.reshape(-1, BLOCK), job_block.reshape(-1).astype(jnp.int32), num_segments=JBLK)
    gradient = totals - capacity.astype(jnp.float32)
    members = jax.ops.segment_sum(row_part.reshape(-1, BLOCK), member_block.reshape(-1).astype(jnp.int32), num_segments=MBLK)
    member_share = members / BLOCK
    return primal.reshape(NBLK, BLOCK, BLOCK), gradient, member_share
```

```python
import functools

import jax
import jax.numpy as jnp
from jax import lax
from jax.experimental import pallas as pl
from jax.experimental.pallas import tpu as pltpu
from jax.sharding import PartitionSpec as P

MB_DEV = 32
PEER_MOST = 9
CHUNK = 8
GROUP = 8
VMEM_LIMIT = 16 << 20

MESH = pl.DeviceIdType.MESH


def high_bit(distance):
    return 1 << (distance.bit_length() - 1)


def partner(index, distance, count):
    assert count & (count - 1) == 0
    bit = 1
    while bit < count:
        flip = (distance // bit) % 2
        index = index + flip * (bit - 2 * bit * ((index // bit) % 2))
        bit *= 2
    return index


def is_lower(index, distance):
    return (index // high_bit(distance)) % 2 == 1


def finish(primal_in, gradient_in, share_in, primal_ref, gradient_ref, share_ref, sem):
    copies = [
        pltpu.make_async_copy(gradient_in, gradient_ref, sem.at[0]),
        pltpu.make_async_copy(share_in, share_ref, sem.at[1]),
    ]
    slots = primal_in.shape[0]
    chunk = min(CHUNK, slots)
    for part in range(slots // chunk):
        rows = pl.ds(part * chunk, chunk)
        copies.append(
            pltpu.make_async_copy(primal_in.at[rows], primal_ref.at[rows], sem.at[2 + part])
        )
    for copy in copies:
        copy.start()
    for copy in copies:
        copy.wait()


def kernel(
    mem_count,
    job_count,
    cost_ref,
    coef_ref,
    member_ref,
    owner_ref,
    local_ref,
    duals_ref,
    capacity_ref,
    primal_ref,
    gradient_ref,
    share_ref,
    cost_v,
    coef_v,
    member_s,
    owner_s,
    local_s,
    capacity_v,
    table,
    block_duals,
    list_v,
    list_s,
    totals,
    incoming,
    member_part,
    member_in,
    load_sem,
    small_sem,
    list_sem,
    mem_enter,
    job_enter,
    gather_send,
    gather_recv,
    column_send,
    column_recv,
    member_send,
    member_recv,
):
    slots, block = cost_v.shape[0], cost_v.shape[1]
    jobs = duals_ref.shape[0]
    chunk = min(CHUNK, slots)
    chunks = slots // chunk
    my_mem = lax.axis_index("mem")
    my_job = lax.axis_index("job")

    barrier = pltpu.get_barrier_semaphore()

    def mem_peer(distance):
        return (partner(my_mem, distance, mem_count), my_job)

    def job_peer(distance):
        return (my_mem, partner(my_job, distance, job_count))

    mem_steps = range(1, mem_count)
    job_steps = range(1, job_count)

    for distance in mem_steps:

        @pl.when(jnp.logical_not(is_lower(my_mem, distance)))
        def _():
            pl.semaphore_signal(
                barrier, inc=1, device_id=mem_peer(distance), device_id_type=MESH
            )

    for distance in job_steps:

        @pl.when(jnp.logical_not(is_lower(my_job, distance)))
        def _():
            pl.semaphore_signal(
                barrier, inc=1, device_id=job_peer(distance), device_id_type=MESH
            )

    @pl.when(my_mem + my_job > 0)
    def _():
        pl.semaphore_wait(barrier, my_mem + my_job)

    for distance in reversed(mem_steps):

        @pl.when(is_lower(my_mem, distance))
        def _():
            pl.semaphore_signal(
                mem_enter.at[distance], inc=1, device_id=mem_peer(distance), device_id_type=MESH
            )

    for distance in reversed(job_steps):

        @pl.when(is_lower(my_job, distance))
        def _():
            pl.semaphore_signal(
                job_enter.at[distance], inc=1, device_id=job_peer(distance), device_id_type=MESH
            )

    small = [
        pltpu.make_async_copy(duals_ref, table.at[my_mem], small_sem.at[0]),
        pltpu.make_async_copy(owner_ref, owner_s, small_sem.at[1]),
        pltpu.make_async_copy(local_ref, local_s, small_sem.at[2]),
        pltpu.make_async_copy(member_ref, member_s, small_sem.at[3]),
        pltpu.make_async_copy(capacity_ref, capacity_v, small_sem.at[4]),
    ]
    for copy in small:
        copy.start()
    loads = []
    for part in range(chunks):
        rows = pl.ds(part * chunk, chunk)
        for index, (source, target) in enumerate(((cost_ref, cost_v), (coef_ref, coef_v))):
            copy = pltpu.make_async_copy(
                source.at[rows], target.at[rows], load_sem.at[2 * part + index]
            )
            copy.start()
            loads.append(copy)
    small[0].wait()

    def gather(distance):
        return pltpu.make_async_remote_copy(
            src_ref=table.at[my_mem],
            dst_ref=table.at[my_mem],
            send_sem=gather_send.at[distance],
            recv_sem=gather_recv.at[distance],
            device_id=mem_peer(distance),
            device_id_type=MESH,
        )

    for distance in reversed(mem_steps):

        @pl.when(is_lower(my_mem, distance))
        def _():
            gather(distance).start()

    small[1].wait()
    small[2].wait()
    owners = lax.broadcasted_iota(jnp.int32, (mem_count, block), 0)
    ranks = lax.broadcasted_iota(jnp.int32, (mem_count, block), 1)

    def enlist(slot, carry):
        slot_list, local_list, count = carry
        hit = owners == owner_s[0, slot]
        put = jnp.logical_and(hit, ranks == count)
        return (
            jnp.where(put, slot, slot_list),
            jnp.where(put, local_s[0, slot], local_list),
            jnp.where(hit, count + 1, count),
        )

    zeros = jnp.zeros((mem_count, block), jnp.int32)
    slot_list, local_list, _ = lax.fori_loop(
        0, slots, enlist, (zeros, zeros - 1, zeros), unroll=4
    )
    list_v[0] = slot_list
    list_v[1] = local_list
    listing = pltpu.make_async_copy(list_v, list_s, list_sem.at[0])
    listing.start()

    for distance in mem_steps:

        @pl.when(jnp.logical_not(is_lower(my_mem, distance)))
        def _():
            pl.semaphore_wait(mem_enter.at[distance], 1)
            gather(distance).start()

    for copy in small[3:]:
        copy.wait()
    for copy in loads:
        copy.wait()
    listing.wait()

    rows_of_block = lax.broadcasted_iota(jnp.int32, (jobs, block), 0)

    def owner_totals(owner):
        block_duals[...] = -table[owner]
        total = jnp.zeros((jobs, block), jnp.float32)
        for rank in range(min(PEER_MOST, slots)):
            slot = list_s[0, owner, rank]
            local = list_s[1, owner, rank]
            dual = block_duals[pl.ds(jnp.maximum(local, 0), 1), :]
            coef = coef_v[slot].astype(jnp.float32)
            allocation = jnp.clip(coef * dual - cost_v[slot].astype(jnp.float32), 0.0, 1.0)
            column = jnp.sum(coef * allocation, axis=0, keepdims=True)
            total = total + jnp.where(rows_of_block == local, column, 0.0)
        return total

    def columns(distance, peer):
        return pltpu.make_async_remote_copy(
            src_ref=totals.at[distance],
            dst_ref=incoming.at[distance],
            send_sem=column_send.at[distance],
            recv_sem=column_recv.at[distance],
            device_id=(peer, my_job),
            device_id_type=MESH,
        )

    totals[0] = owner_totals(my_mem)

    def exchange(distance, carry):
        peer = partner(my_mem, distance, mem_count)
        pltpu.make_async_remote_copy(
            src_ref=table.at[peer],
            dst_ref=table.at[peer],
            send_sem=gather_send.at[distance],
            recv_sem=gather_recv.at[distance],
            device_id=(peer, my_job),
            device_id_type=MESH,
        ).wait_recv()
        totals[distance] = owner_totals(peer)
        columns(distance, peer).start()
        return carry

    lax.fori_loop(1, mem_count, exchange, 0)

    lanes = lax.broadcasted_iota(jnp.int32, (block, block), 1)

    def group(index, members):
        first = GROUP * index
        parts, marks = [], []
        for side in range(GROUP):
            slot = first + side
            dual = -table[owner_s[0, slot], pl.ds(local_s[0, slot], 1), :]
            coef = coef_v[slot].astype(jnp.float32)
            allocation = jnp.clip(coef * dual - cost_v[slot].astype(jnp.float32), 0.0, 1.0)
            part = allocation.astype(jnp.bfloat16)
            primal_ref[slot] = part
            parts.append(part)
            marks.append((lanes == member_s[0, slot]).astype(jnp.float32).astype(jnp.bfloat16))
        return members + jnp.dot(
            jnp.concatenate(parts, axis=1),
            jnp.concatenate(marks, axis=0),
            preferred_element_type=jnp.float32,
        )

    members = lax.fori_loop(
        0, slots // GROUP, group, jnp.zeros((block, block), jnp.float32)
    )
    member_part[...] = members.T[:MB_DEV]

    def shares(distance):
        return pltpu.make_async_remote_copy(
            src_ref=member_part,
            dst_ref=member_in.at[distance],
            send_sem=member_send.at[distance],
            recv_sem=member_recv.at[distance],
            device_id=job_peer(distance),
            device_id_type=MESH,
        )

    for distance in reversed(job_steps):

        @pl.when(jnp.logical_not(is_lower(my_job, distance)))
        def _():
            pl.semaphore_wait(job_enter.at[distance], 1)

        shares(distance).start()

    share = member_part[...]
    for distance in job_steps:
        shares(distance).wait_recv()
        share = share + member_in[distance]
    share_ref[...] = share * (1.0 / block)

    for distance in mem_steps:
        gather(distance).wait_send()
    for distance in job_steps:
        shares(distance).wait_send()
    gradient = totals[0] - capacity_v[...].astype(jnp.float32)
    for distance in mem_steps:
        columns(distance, partner(my_mem, distance, mem_count)).wait_send()
    for distance in mem_steps:
        columns(distance, partner(my_mem, distance, mem_count)).wait_recv()
        gradient = gradient + incoming[distance]
    gradient_ref[...] = gradient


def solution(mesh):
    mem_count, job_count = mesh.shape["mem"], mesh.shape["job"]
    row = P(("mem", "job"))

    def per_device(pair_cost, pair_coef, slot_member, slot_owner, slot_local, duals, capacity):
        slots, block, _ = pair_cost.shape
        jobs = duals.shape[0]
        chunks = slots // min(CHUNK, slots)
        hbm = pl.BlockSpec(memory_space=pltpu.HBM)
        vmem = pl.BlockSpec(memory_space=pltpu.VMEM)
        dma = pltpu.SemaphoreType.DMA
        regular = pltpu.SemaphoreType.REGULAR
        out_shape = (
            jax.ShapeDtypeStruct(pair_cost.shape, jnp.bfloat16),
            jax.ShapeDtypeStruct((jobs, block), jnp.float32),
            jax.ShapeDtypeStruct((MB_DEV, block), jnp.float32),
        )
        operands = (
            pair_cost,
            pair_coef,
            slot_member,
            slot_owner.reshape(1, slots),
            slot_local,
            duals,
            capacity,
        )
        operands = [pltpu.with_memory_space_constraint(value, pltpu.HBM) for value in operands]
        results = pl.pallas_call(
            functools.partial(kernel, mem_count, job_count),
            out_shape=out_shape,
            in_specs=[hbm] * 7,
            out_specs=(vmem,) * 3,
            scratch_shapes=[
                pltpu.VMEM(pair_cost.shape, jnp.bfloat16),
                pltpu.VMEM(pair_cost.shape, jnp.bfloat16),
                pltpu.SMEM((1, slots), jnp.int32),
                pltpu.SMEM((1, slots), jnp.int32),
                pltpu.SMEM((1, slots), jnp.int32),
                pltpu.VMEM((jobs, block), jnp.int32),
                pltpu.VMEM((mem_count, jobs, block), jnp.float32),
                pltpu.VMEM((jobs, block), jnp.float32),
                pltpu.VMEM((2, mem_count, block), jnp.int32),
                pltpu.SMEM((2, mem_count, block), jnp.int32),
                pltpu.VMEM((mem_count, jobs, block), jnp.float32),
                pltpu.VMEM((mem_count, jobs, block), jnp.float32),
                pltpu.VMEM((MB_DEV, block), jnp.float32),
                pltpu.VMEM((job_count, MB_DEV, block), jnp.float32),
                dma((2 * chunks,)),
                dma((5,)),
                dma((1,)),
                regular((mem_count,)),
                regular((job_count,)),
                dma((mem_count,)),
                dma((mem_count,)),
                dma((mem_count,)),
                dma((mem_count,)),
                dma((job_count,)),
                dma((job_count,)),
            ],
            compiler_params=pltpu.CompilerParams(
                collective_id=0, has_side_effects=True, vmem_limit_bytes=VMEM_LIMIT
            ),
        )(*operands)
        return pl.pallas_call(
            finish,
            out_shape=out_shape,
            in_specs=[pl.BlockSpec(memory_space=pl.ANY)] * 3,
            out_specs=(hbm,) * 3,
            scratch_shapes=[dma((2 + chunks,))],
            compiler_params=pltpu.CompilerParams(vmem_limit_bytes=VMEM_LIMIT),
        )(*results)

    return jax.shard_map(
        per_device,
        mesh=mesh,
        in_specs=(row,) * 7,
        out_specs=(row, row, P("mem")),
        check_vma=False,
    )
```

```python
import functools

import jax
import jax.numpy as jnp
from jax import lax
from jax.experimental import pallas as pl
from jax.experimental.pallas import tpu as pltpu
from jax.sharding import PartitionSpec as P

MB_DEV = 32
PEER_MOST = 9
CHUNK = 8
GROUP = 8
VMEM_LIMIT = 16 << 20

MESH = pl.DeviceIdType.MESH


def partner(index, distance, count):
    assert count & (count - 1) == 0
    bit = 1
    while bit < count:
        flip = (distance // bit) % 2
        index = index + flip * (bit - 2 * bit * ((index // bit) % 2))
        bit *= 2
    return index


def finish(primal_in, gradient_in, share_in, primal_ref, gradient_ref, share_ref, sem):
    copies = [
        pltpu.make_async_copy(gradient_in, gradient_ref, sem.at[0]),
        pltpu.make_async_copy(share_in, share_ref, sem.at[1]),
    ]
    slots = primal_in.shape[0]
    chunk = min(CHUNK, slots)
    for part in range(slots // chunk):
        rows = pl.ds(part * chunk, chunk)
        copies.append(
            pltpu.make_async_copy(primal_in.at[rows], primal_ref.at[rows], sem.at[2 + part])
        )
    for copy in copies:
        copy.start()
    for copy in copies:
        copy.wait()


def kernel(
    mem_count,
    job_count,
    cost_ref,
    coef_ref,
    member_ref,
    owner_ref,
    local_ref,
    duals_ref,
    capacity_ref,
    primal_ref,
    gradient_ref,
    share_ref,
    cost_v,
    coef_v,
    member_s,
    owner_s,
    local_s,
    owner_v,
    local_v,
    capacity_v,
    table,
    proxy,
    head_duals,
    list_v,
    list_s,
    match_v,
    column,
    totals,
    head_total,
    incoming,
    member_part,
    member_in,
    load_sem,
    small_sem,
    list_sem,
    proxy_send,
    proxy_recv,
    gather_send,
    gather_recv,
    column_send,
    column_recv,
    member_send,
    member_recv,
):
    slots, block = cost_v.shape[0], cost_v.shape[1]
    jobs = duals_ref.shape[0]
    chunk = min(CHUNK, slots)
    chunks = slots // chunk
    my_mem = lax.axis_index("mem")
    my_job = lax.axis_index("job")
    other_job = partner(my_job, 1, job_count)
    is_head = my_mem == 0
    is_proxy = my_mem == 1
    mem_steps = range(1, mem_count)
    job_steps = range(1, job_count)

    barrier = pltpu.get_barrier_semaphore()

    def greet(*peer):
        pl.semaphore_signal(barrier, inc=1, device_id=peer, device_id_type=MESH)

    def mem_peer(distance):
        return partner(my_mem, distance, mem_count)

    def job_peer(distance):
        return partner(my_job, distance, job_count)

    @pl.when(my_mem > 1)
    def _():
        greet(1, other_job)

    @pl.when(is_proxy)
    def _():
        greet(0, other_job)

    for distance in reversed(mem_steps):
        peer = mem_peer(distance)

        @pl.when(peer > 0)
        def _():
            greet(peer, my_job)

    for distance in reversed(job_steps):
        greet(my_mem, job_peer(distance))

    small = [
        pltpu.make_async_copy(duals_ref, table.at[my_mem], small_sem.at[0]),
        pltpu.make_async_copy(owner_ref, owner_s, small_sem.at[1]),
        pltpu.make_async_copy(local_ref, local_s, small_sem.at[2]),
        pltpu.make_async_copy(owner_ref, owner_v, small_sem.at[3]),
        pltpu.make_async_copy(local_ref, local_v, small_sem.at[4]),
        pltpu.make_async_copy(member_ref, member_s, small_sem.at[5]),
        pltpu.make_async_copy(capacity_ref, capacity_v, small_sem.at[6]),
    ]
    for copy in small:
        copy.start()
    loads = []
    for part in range(chunks):
        rows = pl.ds(part * chunk, chunk)
        for index, (source, target) in enumerate(((cost_ref, cost_v), (coef_ref, coef_v))):
            copy = pltpu.make_async_copy(
                source.at[rows], target.at[rows], load_sem.at[2 * part + index]
            )
            copy.start()
            loads.append(copy)
    small[0].wait()

    def to_proxy():
        return pltpu.make_async_remote_copy(
            src_ref=table.at[0],
            dst_ref=proxy,
            send_sem=proxy_send.at[0],
            recv_sem=proxy_recv.at[0],
            device_id=(1, other_job),
            device_id_type=MESH,
        )

    def from_proxy(mem):
        return pltpu.make_async_remote_copy(
            src_ref=proxy,
            dst_ref=table.at[0],
            send_sem=proxy_send.at[mem],
            recv_sem=gather_recv.at[mem],
            device_id=(mem, other_job),
            device_id_type=MESH,
        )

    def gather(distance):
        return pltpu.make_async_remote_copy(
            src_ref=table.at[my_mem],
            dst_ref=table.at[my_mem],
            send_sem=gather_send.at[distance],
            recv_sem=gather_recv.at[distance],
            device_id=(mem_peer(distance), my_job),
            device_id_type=MESH,
        )

    @pl.when(is_head)
    def _():
        pl.semaphore_wait(barrier, job_count)
        to_proxy().start()

    small[1].wait()
    small[2].wait()
    ranks = lax.broadcasted_iota(jnp.int32, (8, block), 1)

    def enlist(slot, carry):
        slot_list, local_list, count = carry
        hit = owner_s[0, slot] == 0
        put = ranks == jnp.where(hit, count, -1)
        return (
            jnp.where(put, slot, slot_list),
            jnp.where(put, local_s[0, slot], local_list),
            count + hit.astype(jnp.int32),
        )

    zeros = jnp.zeros((8, block), jnp.int32)
    slot_list, local_list, _ = lax.fori_loop(
        0, slots, enlist, (zeros, zeros - 1, jnp.int32(0)), unroll=4
    )
    list_v[0] = slot_list
    list_v[1] = local_list
    listing = pltpu.make_async_copy(list_v, list_s, list_sem.at[0])
    listing.start()

    small[3].wait()
    small[4].wait()
    named = owner_v[...] * jobs + local_v[...]
    match = lax.broadcasted_iota(jnp.int32, (mem_count * jobs, slots), 0) == named
    match_v[...] = match.astype(jnp.float32).astype(jnp.bfloat16)

    @pl.when(is_proxy)
    def _():
        pl.semaphore_wait(barrier, 2 * mem_count + job_count - 4)
        to_proxy().wait_recv()
        for mem in reversed(mem_steps):
            from_proxy(mem).start()

    @pl.when(my_mem > 1)
    def _():
        pl.semaphore_wait(barrier, mem_count + job_count - 2)

    @pl.when(jnp.logical_not(is_head))
    def _():
        for distance in reversed(mem_steps):
            gather(distance).start()

    for copy in small[5:]:
        copy.wait()
    for copy in loads:
        copy.wait()
    listing.wait()

    rows_of_block = lax.broadcasted_iota(jnp.int32, (jobs, block), 0)

    def columns(source, distance, peer):
        return pltpu.make_async_remote_copy(
            src_ref=source,
            dst_ref=incoming.at[distance],
            send_sem=column_send.at[distance],
            recv_sem=column_recv.at[distance],
            device_id=(peer, my_job),
            device_id_type=MESH,
        )

    def columns_to(distance):
        peer = mem_peer(distance)
        rows = pl.ds(pl.multiple_of(peer * jobs, jobs), jobs)
        return columns(totals.at[rows], distance, peer)

    def allocate(slot, dual):
        coef = coef_v[slot].astype(jnp.float32)
        allocation = jnp.clip(coef * dual - cost_v[slot].astype(jnp.float32), 0.0, 1.0)
        return allocation, jnp.sum(coef * allocation, axis=0, keepdims=True)

    @pl.when(jnp.logical_not(is_head))
    def _():
        pltpu.make_async_remote_copy(
            src_ref=table.at[0],
            dst_ref=table.at[0],
            send_sem=gather_send.at[my_mem],
            recv_sem=gather_recv.at[my_mem],
            device_id=(0, my_job),
            device_id_type=MESH,
        ).wait_recv()
        head_duals[...] = -table[0]
        total = jnp.zeros((jobs, block), jnp.float32)
        for rank in range(min(PEER_MOST, slots)):
            slot = list_s[0, 0, rank]
            local = list_s[1, 0, rank]
            dual = head_duals[pl.ds(jnp.maximum(local, 0), 1), :]
            total = total + jnp.where(rows_of_block == local, allocate(slot, dual)[1], 0.0)
        head_total[...] = total
        columns(head_total, my_mem, 0).start()

    for distance in mem_steps:

        @pl.when(distance != my_mem)
        def _():
            gather(distance).wait_recv()

    member_rows = lax.broadcasted_iota(jnp.int32, (MB_DEV, block), 0)

    def group(index, members):
        parts, marks = [], []
        for side in range(GROUP):
            slot = GROUP * index + side
            dual = -table[owner_s[0, slot], pl.ds(local_s[0, slot], 1), :]
            allocation, sums = allocate(slot, dual)
            part = allocation.astype(jnp.bfloat16)
            primal_ref[slot] = part
            column[pl.ds(slot, 1), :] = sums
            mark = (member_rows == member_s[0, slot]).astype(jnp.float32).astype(jnp.bfloat16)
            parts.append(part)
            marks.append(mark)
        return members + lax.dot_general(
            jnp.concatenate(marks, axis=1),
            jnp.concatenate(parts, axis=1),
            (((1,), (1,)), ((), ())),
            preferred_element_type=jnp.float32,
        )

    members = lax.fori_loop(
        0, slots // GROUP, group, jnp.zeros((MB_DEV, block), jnp.float32), unroll=True
    )

    match = match_v[...]
    sums = column[...]
    high = sums.astype(jnp.bfloat16)
    low = (sums - high.astype(jnp.float32)).astype(jnp.bfloat16)
    totals[...] = jnp.dot(match, high, preferred_element_type=jnp.float32) + jnp.dot(
        match, low, preferred_element_type=jnp.float32
    )
    for distance in reversed(mem_steps):

        @pl.when(distance != my_mem)
        def _():
            columns_to(distance).start()

    member_part[...] = members

    def shares(distance):
        return pltpu.make_async_remote_copy(
            src_ref=member_part,
            dst_ref=member_in.at[distance],
            send_sem=member_send.at[distance],
            recv_sem=member_recv.at[distance],
            device_id=(my_mem, job_peer(distance)),
            device_id_type=MESH,
        )

    for distance in reversed(job_steps):
        shares(distance).start()

    own_rows = pl.ds(pl.multiple_of(my_mem * jobs, jobs), jobs)
    gradient = totals[own_rows, :] - capacity_v[...].astype(jnp.float32)

    @pl.when(is_head)
    def _():
        to_proxy().wait_send()

    @pl.when(is_proxy)
    def _():
        for mem in mem_steps:
            from_proxy(mem).wait_send()

    @pl.when(jnp.logical_not(is_head))
    def _():
        for distance in mem_steps:
            gather(distance).wait_send()

    share = member_part[...]
    for distance in job_steps:
        shares(distance).wait_recv()
        share = share + member_in[distance]
    share_ref[...] = share * (1.0 / block)
    for distance in job_steps:
        shares(distance).wait_send()
    for distance in mem_steps:
        columns_to(distance).wait_send()
    for distance in mem_steps:
        columns_to(distance).wait_recv()
        gradient = gradient + incoming[distance]
    gradient_ref[...] = gradient


def solution(mesh):
    mem_count, job_count = mesh.shape["mem"], mesh.shape["job"]
    row = P(("mem", "job"))

    def per_device(pair_cost, pair_coef, slot_member, slot_owner, slot_local, duals, capacity):
        slots, block, _ = pair_cost.shape
        jobs = duals.shape[0]
        chunks = slots // min(CHUNK, slots)
        hbm = pl.BlockSpec(memory_space=pltpu.HBM)
        vmem = pl.BlockSpec(memory_space=pltpu.VMEM)
        dma = pltpu.SemaphoreType.DMA
        out_shape = (
            jax.ShapeDtypeStruct(pair_cost.shape, jnp.bfloat16),
            jax.ShapeDtypeStruct((jobs, block), jnp.float32),
            jax.ShapeDtypeStruct((MB_DEV, block), jnp.float32),
        )
        operands = (
            pair_cost,
            pair_coef,
            slot_member,
            slot_owner.reshape(1, slots),
            slot_local,
            duals,
            capacity,
        )
        operands = [pltpu.with_memory_space_constraint(value, pltpu.HBM) for value in operands]
        results = pl.pallas_call(
            functools.partial(kernel, mem_count, job_count),
            out_shape=out_shape,
            in_specs=[hbm] * 7,
            out_specs=(vmem,) * 3,
            scratch_shapes=[
                pltpu.VMEM(pair_cost.shape, jnp.bfloat16),
                pltpu.VMEM(pair_cost.shape, jnp.bfloat16),
                pltpu.SMEM((1, slots), jnp.int32),
                pltpu.SMEM((1, slots), jnp.int32),
                pltpu.SMEM((1, slots), jnp.int32),
                pltpu.VMEM((1, slots), jnp.int32),
                pltpu.VMEM((1, slots), jnp.int32),
                pltpu.VMEM((jobs, block), jnp.int32),
                pltpu.VMEM((mem_count, jobs, block), jnp.float32),
                pltpu.VMEM((jobs, block), jnp.float32),
                pltpu.VMEM((jobs, block), jnp.float32),
                pltpu.VMEM((2, 8, block), jnp.int32),
                pltpu.SMEM((2, 8, block), jnp.int32),
                pltpu.VMEM((mem_count * jobs, slots), jnp.bfloat16),
                pltpu.VMEM((slots, block), jnp.float32),
                pltpu.VMEM((mem_count * jobs, block), jnp.float32),
                pltpu.VMEM((jobs, block), jnp.float32),
                pltpu.VMEM((mem_count, jobs, block), jnp.float32),
                pltpu.VMEM((MB_DEV, block), jnp.float32),
                pltpu.VMEM((job_count, MB_DEV, block), jnp.float32),
                dma((2 * chunks,)),
                dma((7,)),
                dma((1,)),
                dma((mem_count,)),
                dma((1,)),
                dma((mem_count,)),
                dma((mem_count,)),
                dma((mem_count,)),
                dma((mem_count,)),
                dma((job_count,)),
                dma((job_count,)),
            ],
            compiler_params=pltpu.CompilerParams(
                collective_id=0, has_side_effects=True, vmem_limit_bytes=VMEM_LIMIT
            ),
        )(*operands)
        return pl.pallas_call(
            finish,
            out_shape=out_shape,
            in_specs=[pl.BlockSpec(memory_space=pl.ANY)] * 3,
            out_specs=(hbm,) * 3,
            scratch_shapes=[dma((2 + chunks,))],
            compiler_params=pltpu.CompilerParams(vmem_limit_bytes=VMEM_LIMIT),
        )(*results)

    return jax.shard_map(
        per_device,
        mesh=mesh,
        in_specs=(row,) * 7,
        out_specs=(row, row, P("mem")),
        check_vma=False,
    )
```

```python
import functools

import jax
import jax.numpy as jnp
from jax import lax
from jax.experimental import pallas as pl
from jax.experimental.pallas import tpu as pltpu
from jax.sharding import PartitionSpec as P

MB_DEV = 32
PEER_MOST = 9
FIRST = 2
CHUNK = 8
GROUP = 8
VMEM_LIMIT = 16 << 20

MESH = pl.DeviceIdType.MESH


def partner(index, distance, count):
    assert count & (count - 1) == 0
    bit = 1
    while bit < count:
        flip = (distance // bit) % 2
        index = index + flip * (bit - 2 * bit * ((index // bit) % 2))
        bit *= 2
    return index


def finish(primal_in, gradient_in, share_in, primal_ref, gradient_ref, share_ref, sem):
    copies = [
        pltpu.make_async_copy(gradient_in, gradient_ref, sem.at[0]),
        pltpu.make_async_copy(share_in, share_ref, sem.at[1]),
    ]
    slots = primal_in.shape[0]
    chunk = min(CHUNK, slots)
    for part in range(slots // chunk):
        rows = pl.ds(part * chunk, chunk)
        copies.append(
            pltpu.make_async_copy(primal_in.at[rows], primal_ref.at[rows], sem.at[2 + part])
        )
    for copy in copies:
        copy.start()
    for copy in copies:
        copy.wait()


def kernel(
    mem_count,
    job_count,
    cost_ref,
    coef_ref,
    member_ref,
    owner_ref,
    local_ref,
    duals_ref,
    capacity_ref,
    primal_ref,
    gradient_ref,
    share_ref,
    cost_v,
    coef_v,
    cost_w,
    coef_w,
    member_s,
    owner_s,
    local_s,
    owner_v,
    local_v,
    capacity_v,
    table,
    proxy,
    first_duals,
    list_v,
    list_s,
    match_v,
    column,
    totals,
    first_totals,
    incoming,
    member_part,
    member_in,
    load_sem,
    small_sem,
    list_sem,
    proxy_send,
    proxy_recv,
    gather_send,
    gather_recv,
    column_send,
    column_recv,
    member_send,
    member_recv,
):
    slots, block = cost_v.shape[0], cost_v.shape[1]
    jobs = duals_ref.shape[0]
    chunk = min(CHUNK, slots)
    chunks = slots // chunk
    my_mem = lax.axis_index("mem")
    my_job = lax.axis_index("job")
    is_head = my_mem == 0
    is_proxy = my_mem == 1
    mem_steps = range(1, mem_count)
    job_steps = range(1, job_count)

    barrier = pltpu.get_barrier_semaphore()

    def greet(*peer):
        pl.semaphore_signal(barrier, inc=1, device_id=peer, device_id_type=MESH)

    def flips(index, count):
        bits = range(count.bit_length() - 1)
        return [(1 << bit) - (2 << bit) * ((index // (1 << bit)) % 2) for bit in bits]

    mem_flips = flips(my_mem, mem_count)
    job_flips = flips(my_job, job_count)

    def mem_peer(distance):
        return my_mem + sum(flip for bit, flip in enumerate(mem_flips) if distance >> bit & 1)

    def job_peer(distance):
        return my_job + sum(flip for bit, flip in enumerate(job_flips) if distance >> bit & 1)

    other_job = job_peer(1)

    @pl.when(my_mem > 1)
    def _():
        greet(1, other_job)

    @pl.when(is_proxy)
    def _():
        greet(0, other_job)

    for distance in mem_steps:
        peer = mem_peer(distance)

        @pl.when(peer > 0)
        def _():
            greet(peer, my_job)

    for distance in reversed(job_steps):
        greet(my_mem, job_peer(distance))

    small = [
        pltpu.make_async_copy(duals_ref, table.at[my_mem], small_sem.at[0]),
        pltpu.make_async_copy(owner_ref, owner_s, small_sem.at[1]),
        pltpu.make_async_copy(local_ref, local_s, small_sem.at[2]),
        pltpu.make_async_copy(owner_ref, owner_v, small_sem.at[3]),
        pltpu.make_async_copy(local_ref, local_v, small_sem.at[4]),
        pltpu.make_async_copy(member_ref, member_s, small_sem.at[5]),
        pltpu.make_async_copy(capacity_ref, capacity_v, small_sem.at[6]),
    ]
    for copy in small:
        copy.start()
    loads = []
    for part in range(chunks):
        rows = pl.ds(part * chunk, chunk)
        for index, (source, target) in enumerate(((cost_ref, cost_v), (coef_ref, coef_v))):
            copy = pltpu.make_async_copy(
                source.at[rows], target.at[rows], load_sem.at[2 * part + index]
            )
            copy.start()
            loads.append(copy)
    small[0].wait()

    def to_proxy():
        return pltpu.make_async_remote_copy(
            src_ref=table.at[0],
            dst_ref=proxy,
            send_sem=proxy_send.at[0],
            recv_sem=proxy_recv.at[0],
            device_id=(1, other_job),
            device_id_type=MESH,
        )

    def from_proxy(mem):
        return pltpu.make_async_remote_copy(
            src_ref=proxy,
            dst_ref=table.at[0],
            send_sem=proxy_send.at[mem],
            recv_sem=gather_recv.at[mem],
            device_id=(mem, other_job),
            device_id_type=MESH,
        )

    def gather(distance):
        return pltpu.make_async_remote_copy(
            src_ref=table.at[my_mem],
            dst_ref=table.at[my_mem],
            send_sem=gather_send.at[distance],
            recv_sem=gather_recv.at[distance],
            device_id=(mem_peer(distance), my_job),
            device_id_type=MESH,
        )

    @pl.when(is_head)
    def _():
        pl.semaphore_wait(barrier, job_count)
        to_proxy().start()

    small[1].wait()
    small[2].wait()
    owners = lax.broadcasted_iota(jnp.int32, (8, block), 0)
    ranks = lax.broadcasted_iota(jnp.int32, (8, block), 1)

    def enlist(slot, carry):
        slot_list, local_list, count = carry
        hit = owners == owner_s[0, slot]
        put = jnp.logical_and(hit, ranks == count)
        return (
            jnp.where(put, slot, slot_list),
            jnp.where(put, local_s[0, slot], local_list),
            jnp.where(hit, count + 1, count),
        )

    zeros = jnp.zeros((8, block), jnp.int32)
    slot_list, local_list, _ = lax.fori_loop(
        0, slots, enlist, (zeros, zeros - 1, zeros), unroll=4
    )
    list_v[0] = slot_list
    list_v[1] = local_list
    listing = pltpu.make_async_copy(list_v, list_s, list_sem.at[0])
    listing.start()

    small[3].wait()
    small[4].wait()
    named = owner_v[...] * jobs + local_v[...]
    match = lax.broadcasted_iota(jnp.int32, (mem_count * jobs, slots), 0) == named
    match_v[...] = match.astype(jnp.float32).astype(jnp.bfloat16)

    @pl.when(is_proxy)
    def _():
        pl.semaphore_wait(barrier, 2 * mem_count + job_count - 4)
        to_proxy().wait_recv()
        for step in reversed(mem_steps):
            from_proxy(step).start()
            gather(step).start()

    @pl.when(my_mem > 1)
    def _():
        pl.semaphore_wait(barrier, mem_count + job_count - 2)
        for distance in reversed(mem_steps):
            gather(distance).start()

    for copy in small[5:]:
        copy.wait()
    for copy in loads:
        copy.wait()
    listing.wait()

    def widen(slot, carry):
        cost_w[slot] = cost_v[slot].astype(jnp.float32)
        coef_w[slot] = coef_v[slot].astype(jnp.float32)
        return carry

    lax.fori_loop(0, slots, widen, 0, unroll=2)

    rows_of_block = lax.broadcasted_iota(jnp.int32, (jobs, block), 0)

    def columns(source, distance, peer):
        return pltpu.make_async_remote_copy(
            src_ref=source,
            dst_ref=incoming.at[distance],
            send_sem=column_send.at[distance],
            recv_sem=column_recv.at[distance],
            device_id=(peer, my_job),
            device_id_type=MESH,
        )

    def columns_to(distance):
        peer = mem_peer(distance)
        rows = pl.ds(pl.multiple_of(peer * jobs, jobs), jobs)
        return columns(totals.at[rows], distance, peer)

    def allocate(slot, dual):
        coef = coef_w[slot]
        allocation = jnp.clip(coef * dual - cost_w[slot], 0.0, 1.0)
        return allocation, jnp.sum(coef * allocation, axis=0, keepdims=True)

    for owner in range(FIRST):

        @pl.when(my_mem > owner)
        def _():
            distance = partner(my_mem, owner, mem_count)
            pltpu.make_async_remote_copy(
                src_ref=table.at[owner],
                dst_ref=table.at[owner],
                send_sem=gather_send.at[distance],
                recv_sem=gather_recv.at[distance],
                device_id=(owner, my_job),
                device_id_type=MESH,
            ).wait_recv()
            first_duals[...] = -table[owner]
            total = jnp.zeros((jobs, block), jnp.float32)
            for rank in range(min(PEER_MOST, slots)):
                slot = list_s[0, owner, rank]
                local = list_s[1, owner, rank]
                dual = first_duals[pl.ds(jnp.maximum(local, 0), 1), :]
                total = total + jnp.where(rows_of_block == local, allocate(slot, dual)[1], 0.0)
            first_totals[owner] = total
            columns(first_totals.at[owner], distance, owner).start()

    def later(distance):
        peer = mem_peer(distance)
        return peer >= jnp.minimum(my_mem, FIRST)

    for distance in mem_steps:

        @pl.when(later(distance))
        def _():
            gather(distance).wait_recv()

    member_rows = lax.broadcasted_iota(jnp.int32, (MB_DEV, block), 0)

    def group(index, members):
        parts, marks = [], []
        for side in range(GROUP):
            slot = GROUP * index + side
            dual = -table[owner_s[0, slot], pl.ds(local_s[0, slot], 1), :]
            allocation, sums = allocate(slot, dual)
            part = allocation.astype(jnp.bfloat16)
            primal_ref[slot] = part
            column[pl.ds(slot, 1), :] = sums
            mark = (member_rows == member_s[0, slot]).astype(jnp.float32).astype(jnp.bfloat16)
            parts.append(part)
            marks.append(mark)
        return members + lax.dot_general(
            jnp.concatenate(marks, axis=1),
            jnp.concatenate(parts, axis=1),
            (((1,), (1,)), ((), ())),
            preferred_element_type=jnp.float32,
        )

    members = lax.fori_loop(
        0, slots // GROUP, group, jnp.zeros((MB_DEV, block), jnp.float32), unroll=True
    )

    match = match_v[...]
    sums = column[...]
    high = sums.astype(jnp.bfloat16)
    low = (sums - high.astype(jnp.float32)).astype(jnp.bfloat16)
    totals[...] = jnp.dot(match, high, preferred_element_type=jnp.float32) + jnp.dot(
        match, low, preferred_element_type=jnp.float32
    )

    member_part[...] = members

    def shares(distance):
        return pltpu.make_async_remote_copy(
            src_ref=member_part,
            dst_ref=member_in.at[distance],
            send_sem=member_send.at[distance],
            recv_sem=member_recv.at[distance],
            device_id=(my_mem, job_peer(distance)),
            device_id_type=MESH,
        )

    def send_columns():
        for distance in reversed(mem_steps):

            @pl.when(later(distance))
            def _():
                columns_to(distance).start()

    @pl.when(jnp.logical_not(is_head))
    def _():
        send_columns()

    for distance in sorted(job_steps, key=lambda step: step % 2):
        shares(distance).start()

    @pl.when(is_head)
    def _():
        send_columns()

    own_rows = pl.ds(pl.multiple_of(my_mem * jobs, jobs), jobs)
    gradient = totals[own_rows, :] - capacity_v[...].astype(jnp.float32)

    @pl.when(is_head)
    def _():
        to_proxy().wait_send()

    @pl.when(is_proxy)
    def _():
        for mem in mem_steps:
            from_proxy(mem).wait_send()

    @pl.when(jnp.logical_not(is_head))
    def _():
        for distance in mem_steps:
            gather(distance).wait_send()

    share = member_part[...]
    for distance in job_steps:
        shares(distance).wait_recv()
        share = share + member_in[distance]
    share_ref[...] = share * (1.0 / block)
    for distance in job_steps:
        shares(distance).wait_send()
    for distance in mem_steps:
        columns_to(distance).wait_send()
    for distance in mem_steps:
        columns_to(distance).wait_recv()
        gradient = gradient + incoming[distance]
    gradient_ref[...] = gradient


def solution(mesh):
    mem_count, job_count = mesh.shape["mem"], mesh.shape["job"]
    row = P(("mem", "job"))

    def per_device(pair_cost, pair_coef, slot_member, slot_owner, slot_local, duals, capacity):
        slots, block, _ = pair_cost.shape
        jobs = duals.shape[0]
        chunks = slots // min(CHUNK, slots)
        hbm = pl.BlockSpec(memory_space=pltpu.HBM)
        vmem = pl.BlockSpec(memory_space=pltpu.VMEM)
        dma = pltpu.SemaphoreType.DMA
        out_shape = (
            jax.ShapeDtypeStruct(pair_cost.shape, jnp.bfloat16),
            jax.ShapeDtypeStruct((jobs, block), jnp.float32),
            jax.ShapeDtypeStruct((MB_DEV, block), jnp.float32),
        )
        operands = (
            pair_cost,
            pair_coef,
            slot_member,
            slot_owner.reshape(1, slots),
            slot_local,
            duals,
            capacity,
        )
        operands = [pltpu.with_memory_space_constraint(value, pltpu.HBM) for value in operands]
        results = pl.pallas_call(
            functools.partial(kernel, mem_count, job_count),
            out_shape=out_shape,
            in_specs=[hbm] * 7,
            out_specs=(vmem,) * 3,
            scratch_shapes=[
                pltpu.VMEM(pair_cost.shape, jnp.bfloat16),
                pltpu.VMEM(pair_cost.shape, jnp.bfloat16),
                pltpu.VMEM(pair_cost.shape, jnp.float32),
                pltpu.VMEM(pair_cost.shape, jnp.float32),
                pltpu.SMEM((1, slots), jnp.int32),
                pltpu.SMEM((1, slots), jnp.int32),
                pltpu.SMEM((1, slots), jnp.int32),
                pltpu.VMEM((1, slots), jnp.int32),
                pltpu.VMEM((1, slots), jnp.int32),
                pltpu.VMEM((jobs, block), jnp.int32),
                pltpu.VMEM((mem_count, jobs, block), jnp.float32),
                pltpu.VMEM((jobs, block), jnp.float32),
                pltpu.VMEM((jobs, block), jnp.float32),
                pltpu.VMEM((2, 8, block), jnp.int32),
                pltpu.SMEM((2, 8, block), jnp.int32),
                pltpu.VMEM((mem_count * jobs, slots), jnp.bfloat16),
                pltpu.VMEM((slots, block), jnp.float32),
                pltpu.VMEM((mem_count * jobs, block), jnp.float32),
                pltpu.VMEM((FIRST, jobs, block), jnp.float32),
                pltpu.VMEM((mem_count, jobs, block), jnp.float32),
                pltpu.VMEM((MB_DEV, block), jnp.float32),
                pltpu.VMEM((job_count, MB_DEV, block), jnp.float32),
                dma((2 * chunks,)),
                dma((7,)),
                dma((1,)),
                dma((mem_count,)),
                dma((1,)),
                dma((mem_count,)),
                dma((mem_count,)),
                dma((mem_count,)),
                dma((mem_count,)),
                dma((job_count,)),
                dma((job_count,)),
            ],
            compiler_params=pltpu.CompilerParams(
                collective_id=0, has_side_effects=True, vmem_limit_bytes=VMEM_LIMIT
            ),
        )(*operands)
        return pl.pallas_call(
            finish,
            out_shape=out_shape,
            in_specs=[pl.BlockSpec(memory_space=pl.ANY)] * 3,
            out_specs=(hbm,) * 3,
            scratch_shapes=[dma((2 + chunks,))],
            compiler_params=pltpu.CompilerParams(vmem_limit_bytes=VMEM_LIMIT),
        )(*results)

    return jax.shard_map(
        per_device,
        mesh=mesh,
        in_specs=(row,) * 7,
        out_specs=(row, row, P("mem")),
        check_vma=False,
    )
```

```python
import functools

import jax
import jax.numpy as jnp
from jax import lax
from jax.experimental import pallas as pl
from jax.experimental.pallas import tpu as pltpu
from jax.sharding import PartitionSpec as P

MB_DEV = 32
PEER_MOST = 9
FIRST = 2
PROXIES = 2
CHUNK = 8
GROUP = 8
VMEM_LIMIT = 16 << 20

MESH = pl.DeviceIdType.MESH


def partner(index, distance, count):
    assert count & (count - 1) == 0
    bit = 1
    while bit < count:
        flip = (distance // bit) % 2
        index = index + flip * (bit - 2 * bit * ((index // bit) % 2))
        bit *= 2
    return index


def finish(primal_in, gradient_in, share_in, primal_ref, gradient_ref, share_ref, sem):
    copies = [
        pltpu.make_async_copy(gradient_in, gradient_ref, sem.at[0]),
        pltpu.make_async_copy(share_in, share_ref, sem.at[1]),
    ]
    slots = primal_in.shape[0]
    chunk = min(CHUNK, slots)
    for part in range(slots // chunk):
        rows = pl.ds(part * chunk, chunk)
        copies.append(
            pltpu.make_async_copy(primal_in.at[rows], primal_ref.at[rows], sem.at[2 + part])
        )
    for copy in copies:
        copy.start()
    for copy in copies:
        copy.wait()


def kernel(
    mem_count,
    job_count,
    cost_ref,
    coef_ref,
    member_ref,
    owner_ref,
    local_ref,
    duals_ref,
    capacity_ref,
    primal_ref,
    gradient_ref,
    share_ref,
    cost_v,
    coef_v,
    cost_w,
    coef_w,
    member_s,
    owner_s,
    local_s,
    owner_v,
    local_v,
    capacity_v,
    table,
    proxy,
    first_duals,
    list_v,
    list_s,
    match_v,
    column,
    totals,
    first_totals,
    incoming,
    member_part,
    member_in,
    load_sem,
    small_sem,
    list_sem,
    job_enter,
    proxy_send,
    proxy_recv,
    gather_send,
    gather_recv,
    column_send,
    column_recv,
    member_send,
    member_recv,
):
    slots, block = cost_v.shape[0], cost_v.shape[1]
    jobs = duals_ref.shape[0]
    my_mem = lax.axis_index("mem")
    my_job = lax.axis_index("job")
    is_head = my_mem == 0
    is_proxy = jnp.logical_and(my_mem > 0, my_mem <= PROXIES)
    mem_steps = range(1, mem_count)
    job_steps = range(1, job_count)

    barrier = pltpu.get_barrier_semaphore()

    def greet(*peer):
        pl.semaphore_signal(barrier, inc=1, device_id=peer, device_id_type=MESH)

    def flips(index, count):
        bits = range(count.bit_length() - 1)
        return [(1 << bit) - (2 << bit) * ((index // (1 << bit)) % 2) for bit in bits]

    mem_flips = flips(my_mem, mem_count)
    job_flips = flips(my_job, job_count)

    def mem_peer(distance):
        return my_mem + sum(flip for bit, flip in enumerate(mem_flips) if distance >> bit & 1)

    def job_peer(distance):
        return my_job + sum(flip for bit, flip in enumerate(job_flips) if distance >> bit & 1)

    other_job = job_peer(1)

    @pl.when(my_mem > PROXIES)
    def _():
        greet(PROXIES - my_mem % 2, other_job)

    @pl.when(is_proxy)
    def _():
        greet(0, other_job)

    for distance in mem_steps:
        peer = mem_peer(distance)

        @pl.when(peer > 0)
        def _():
            greet(peer, my_job)

    for distance in job_steps:
        peer = job_peer(distance)

        @pl.when(jnp.logical_or(my_mem <= PROXIES, peer > my_job))
        def _():
            greet(my_mem, peer)


    small = [
        pltpu.make_async_copy(duals_ref, table.at[my_mem], small_sem.at[0]),
        pltpu.make_async_copy(owner_ref, owner_s, small_sem.at[1]),
        pltpu.make_async_copy(local_ref, local_s, small_sem.at[2]),
        pltpu.make_async_copy(owner_ref, owner_v, small_sem.at[3]),
        pltpu.make_async_copy(local_ref, local_v, small_sem.at[4]),
        pltpu.make_async_copy(member_ref, member_s, small_sem.at[5]),
        pltpu.make_async_copy(capacity_ref, capacity_v, small_sem.at[6]),
    ]
    for copy in small:
        copy.start()
    loads = [
        pltpu.make_async_copy(cost_ref, cost_v, load_sem.at[0]),
        pltpu.make_async_copy(coef_ref, coef_v, load_sem.at[1]),
    ]
    for copy in loads:
        copy.start()
    small[0].wait()

    def to_proxy(mem):
        return pltpu.make_async_remote_copy(
            src_ref=table.at[0],
            dst_ref=proxy,
            send_sem=proxy_send.at[mem],
            recv_sem=proxy_recv.at[0],
            device_id=(mem, other_job),
            device_id_type=MESH,
        )

    def from_proxy(mem):
        return pltpu.make_async_remote_copy(
            src_ref=proxy,
            dst_ref=table.at[0],
            send_sem=proxy_send.at[mem],
            recv_sem=gather_recv.at[mem],
            device_id=(mem, other_job),
            device_id_type=MESH,
        )

    def gather(distance, peer=None):
        peer = mem_peer(distance) if peer is None else peer
        return pltpu.make_async_remote_copy(
            src_ref=table.at[my_mem],
            dst_ref=table.at[my_mem],
            send_sem=gather_send.at[distance],
            recv_sem=gather_recv.at[distance],
            device_id=(peer, my_job),
            device_id_type=MESH,
        )

    @pl.when(is_head)
    def _():
        pl.semaphore_wait(barrier, PROXIES + job_count - 1)
        for mem in range(1, PROXIES + 1):
            to_proxy(mem).start()

    small[1].wait()
    small[2].wait()
    owners = lax.broadcasted_iota(jnp.int32, (8, block), 0)
    ranks = lax.broadcasted_iota(jnp.int32, (8, block), 1)

    def enlist(slot, carry):
        slot_list, local_list, count = carry
        hit = owners == owner_s[0, slot]
        put = jnp.logical_and(hit, ranks == count)
        return (
            jnp.where(put, slot, slot_list),
            jnp.where(put, local_s[0, slot], local_list),
            jnp.where(hit, count + 1, count),
        )

    zeros = jnp.zeros((8, block), jnp.int32)
    slot_list, local_list, _ = lax.fori_loop(
        0, slots, enlist, (zeros, zeros - 1, zeros), unroll=4
    )
    list_v[0] = slot_list
    list_v[1] = local_list
    listing = pltpu.make_async_copy(list_v, list_s, list_sem.at[0])
    listing.start()

    small[3].wait()
    small[4].wait()
    named = owner_v[...] * jobs + local_v[...]
    match = lax.broadcasted_iota(jnp.int32, (mem_count * jobs, slots), 0) == named
    match_v[...] = match.astype(jnp.float32).astype(jnp.bfloat16)

    for mine in range(1, PROXIES + 1):

        @pl.when(my_mem == mine)
        def _():
            served = range(mine, mem_count, PROXIES)
            pl.semaphore_wait(barrier, mem_count + job_count - 3 + len(served))
            to_proxy(mine).wait_recv()
            from_proxy(served[-1]).start()
            gather(mine, 0).start()
            others = [distance for distance in reversed(mem_steps) if distance != mine]
            for place, distance in enumerate(others):
                if place < len(served) - 1:
                    from_proxy(served[-2 - place]).start()
                gather(distance).start()

    @pl.when(my_mem > PROXIES)
    def _():
        pl.semaphore_wait(barrier, mem_count - 1 + my_job)
        gather(my_mem, 0).start()
        for distance in reversed(mem_steps):

            @pl.when(distance != my_mem)
            def _():
                gather(distance).start()

        for distance in job_steps:
            peer = job_peer(distance)

            @pl.when(peer < my_job)
            def _():
                pl.semaphore_signal(
                    job_enter.at[distance],
                    inc=1,
                    device_id=(my_mem, peer),
                    device_id_type=MESH,
                )

    for copy in small[5:]:
        copy.wait()
    for copy in loads:
        copy.wait()
    listing.wait()

    def widen(slot, carry):
        cost_w[slot] = cost_v[slot].astype(jnp.float32)
        coef_w[slot] = coef_v[slot].astype(jnp.float32)
        return carry

    lax.fori_loop(0, slots, widen, 0, unroll=2)

    rows_of_block = lax.broadcasted_iota(jnp.int32, (jobs, block), 0)

    def columns(source, distance, peer):
        return pltpu.make_async_remote_copy(
            src_ref=source,
            dst_ref=incoming.at[distance],
            send_sem=column_send.at[distance],
            recv_sem=column_recv.at[distance],
            device_id=(peer, my_job),
            device_id_type=MESH,
        )

    def columns_to(distance):
        peer = mem_peer(distance)
        rows = pl.ds(pl.multiple_of(peer * jobs, jobs), jobs)
        return columns(totals.at[rows], distance, peer)

    def allocate(slot, dual):
        return jnp.clip(coef_w[slot] * dual - cost_w[slot], 0.0, 1.0)

    def column_sums(slot, allocation):
        return jnp.sum(coef_w[slot] * allocation, axis=0, keepdims=True)

    for owner in range(FIRST):

        @pl.when(my_mem > owner)
        def _():
            distance = partner(my_mem, owner, mem_count)
            pltpu.make_async_remote_copy(
                src_ref=table.at[owner],
                dst_ref=table.at[owner],
                send_sem=gather_send.at[distance],
                recv_sem=gather_recv.at[distance],
                device_id=(owner, my_job),
                device_id_type=MESH,
            ).wait_recv()
            first_duals[...] = -table[owner]
            total = jnp.zeros((jobs, block), jnp.float32)
            for rank in range(min(PEER_MOST, slots)):
                slot = list_s[0, owner, rank]
                local = list_s[1, owner, rank]
                dual = first_duals[pl.ds(jnp.maximum(local, 0), 1), :]
                sums = column_sums(slot, allocate(slot, dual))
                total = total + jnp.where(rows_of_block == local, sums, 0.0)
            first_totals[owner] = total
            columns(first_totals.at[owner], distance, owner).start()

    def later(distance):
        peer = mem_peer(distance)
        return peer >= jnp.minimum(my_mem, FIRST)

    for distance in mem_steps:

        @pl.when(later(distance))
        def _():
            gather(distance).wait_recv()

    member_rows = lax.broadcasted_iota(jnp.int32, (MB_DEV, block), 0)

    def allocate_all(keep):
        def group(index, members):
            parts, marks = [], []
            for side in range(GROUP):
                slot = GROUP * index + side
                dual = -table[owner_s[0, slot], pl.ds(local_s[0, slot], 1), :]
                allocation = allocate(slot, dual)
                part = allocation.astype(jnp.bfloat16)
                primal_ref[slot] = part
                keep(slot, allocation)
                mark = (member_rows == member_s[0, slot]).astype(jnp.float32)
                parts.append(part)
                marks.append(mark.astype(jnp.bfloat16))
            return members + lax.dot_general(
                jnp.concatenate(marks, axis=1),
                jnp.concatenate(parts, axis=1),
                (((1,), (1,)), ((), ())),
                preferred_element_type=jnp.float32,
            )

        member_part[...] = lax.fori_loop(
            0, slots // GROUP, group, jnp.zeros((MB_DEV, block), jnp.float32), unroll=True
        )

    def keep_sums(slot, allocation):
        column[pl.ds(slot, 1), :] = column_sums(slot, allocation)

    def keep_allocation(slot, allocation):
        cost_w[slot] = allocation

    def send_columns():
        match = match_v[...]
        sums = column[...]
        high = sums.astype(jnp.bfloat16)
        low = (sums - high.astype(jnp.float32)).astype(jnp.bfloat16)
        totals[...] = jnp.dot(match, high, preferred_element_type=jnp.float32) + jnp.dot(
            match, low, preferred_element_type=jnp.float32
        )
        for distance in reversed(mem_steps):

            @pl.when(later(distance))
            def _():
                columns_to(distance).start()

    def shares(distance):
        return pltpu.make_async_remote_copy(
            src_ref=member_part,
            dst_ref=member_in.at[distance],
            send_sem=member_send.at[distance],
            recv_sem=member_recv.at[distance],
            device_id=(my_mem, job_peer(distance)),
            device_id_type=MESH,
        )

    def send_shares():
        for distance in sorted(job_steps, key=lambda step: step % 2):

            @pl.when(jnp.logical_and(my_mem > PROXIES, job_peer(distance) > my_job))
            def _():
                pl.semaphore_wait(job_enter.at[distance], 1)

            shares(distance).start()

    @pl.when(is_head)
    def _():
        allocate_all(keep_allocation)
        send_shares()

        def sum_up(slot, carry):
            keep_sums(slot, cost_w[slot])
            return carry

        lax.fori_loop(0, slots, sum_up, 0, unroll=GROUP)
        send_columns()

    @pl.when(jnp.logical_not(is_head))
    def _():
        allocate_all(keep_sums)
        send_columns()
        send_shares()

    own_rows = pl.ds(pl.multiple_of(my_mem * jobs, jobs), jobs)
    gradient = totals[own_rows, :] - capacity_v[...].astype(jnp.float32)

    @pl.when(is_head)
    def _():
        for mem in range(1, PROXIES + 1):
            to_proxy(mem).wait_send()

    for mine in range(1, PROXIES + 1):

        @pl.when(my_mem == mine)
        def _():
            for mem in range(mine, mem_count, PROXIES):
                from_proxy(mem).wait_send()

    @pl.when(jnp.logical_not(is_head))
    def _():
        for distance in mem_steps:
            gather(distance).wait_send()

    share = member_part[...]
    for distance in job_steps:
        shares(distance).wait_recv()
        share = share + member_in[distance]
    share_ref[...] = share * (1.0 / block)
    for distance in job_steps:
        shares(distance).wait_send()
    for distance in mem_steps:
        columns_to(distance).wait_send()
    for distance in mem_steps:
        columns_to(distance).wait_recv()
        gradient = gradient + incoming[distance]
    gradient_ref[...] = gradient


def solution(mesh):
    mem_count, job_count = mesh.shape["mem"], mesh.shape["job"]
    row = P(("mem", "job"))

    def per_device(pair_cost, pair_coef, slot_member, slot_owner, slot_local, duals, capacity):
        slots, block, _ = pair_cost.shape
        jobs = duals.shape[0]
        chunks = slots // min(CHUNK, slots)
        hbm = pl.BlockSpec(memory_space=pltpu.HBM)
        vmem = pl.BlockSpec(memory_space=pltpu.VMEM)
        dma = pltpu.SemaphoreType.DMA
        out_shape = (
            jax.ShapeDtypeStruct(pair_cost.shape, jnp.bfloat16),
            jax.ShapeDtypeStruct((jobs, block), jnp.float32),
            jax.ShapeDtypeStruct((MB_DEV, block), jnp.float32),
        )
        operands = (
            pair_cost,
            pair_coef,
            slot_member,
            slot_owner.reshape(1, slots),
            slot_local,
            duals,
            capacity,
        )
        operands = [pltpu.with_memory_space_constraint(value, pltpu.HBM) for value in operands]
        results = pl.pallas_call(
            functools.partial(kernel, mem_count, job_count),
            out_shape=out_shape,
            in_specs=[hbm] * 7,
            out_specs=(vmem,) * 3,
            scratch_shapes=[
                pltpu.VMEM(pair_cost.shape, jnp.bfloat16),
                pltpu.VMEM(pair_cost.shape, jnp.bfloat16),
                pltpu.VMEM(pair_cost.shape, jnp.float32),
                pltpu.VMEM(pair_cost.shape, jnp.float32),
                pltpu.SMEM((1, slots), jnp.int32),
                pltpu.SMEM((1, slots), jnp.int32),
                pltpu.SMEM((1, slots), jnp.int32),
                pltpu.VMEM((1, slots), jnp.int32),
                pltpu.VMEM((1, slots), jnp.int32),
                pltpu.VMEM((jobs, block), jnp.int32),
                pltpu.VMEM((mem_count, jobs, block), jnp.float32),
                pltpu.VMEM((jobs, block), jnp.float32),
                pltpu.VMEM((jobs, block), jnp.float32),
                pltpu.VMEM((2, 8, block), jnp.int32),
                pltpu.SMEM((2, 8, block), jnp.int32),
                pltpu.VMEM((mem_count * jobs, slots), jnp.bfloat16),
                pltpu.VMEM((slots, block), jnp.float32),
                pltpu.VMEM((mem_count * jobs, block), jnp.float32),
                pltpu.VMEM((FIRST, jobs, block), jnp.float32),
                pltpu.VMEM((mem_count, jobs, block), jnp.float32),
                pltpu.VMEM((MB_DEV, block), jnp.float32),
                pltpu.VMEM((job_count, MB_DEV, block), jnp.float32),
                dma((2,)),
                dma((7,)),
                dma((1,)),
                pltpu.SemaphoreType.REGULAR((job_count,)),
                dma((mem_count,)),
                dma((1,)),
                dma((mem_count,)),
                dma((mem_count,)),
                dma((mem_count,)),
                dma((mem_count,)),
                dma((job_count,)),
                dma((job_count,)),
            ],
            compiler_params=pltpu.CompilerParams(
                collective_id=0, has_side_effects=True, vmem_limit_bytes=VMEM_LIMIT
            ),
        )(*operands)
        return pl.pallas_call(
            finish,
            out_shape=out_shape,
            in_specs=[pl.BlockSpec(memory_space=pl.ANY)] * 3,
            out_specs=(hbm,) * 3,
            scratch_shapes=[dma((2 + chunks,))],
            compiler_params=pltpu.CompilerParams(vmem_limit_bytes=VMEM_LIMIT),
        )(*results)

    return jax.shard_map(
        per_device,
        mesh=mesh,
        in_specs=(row,) * 7,
        out_specs=(row, row, P("mem")),
        check_vma=False,
    )
```

```python
import functools

import jax
import jax.numpy as jnp
from jax import lax
from jax.experimental import pallas as pl
from jax.experimental.pallas import tpu as pltpu
from jax.sharding import PartitionSpec as P

MB_DEV = 32
PEER_MOST = 9
FIRST = 2
PROXIES = 2
GROUP = 8
VMEM_LIMIT = 16 << 20

MESH = pl.DeviceIdType.MESH


def partner(index, distance, count):
    assert count & (count - 1) == 0
    bit = 1
    while bit < count:
        flip = (distance // bit) % 2
        index = index + flip * (bit - 2 * bit * ((index // bit) % 2))
        bit *= 2
    return index


def finish(primal_in, gradient_in, share_in, primal_ref, gradient_ref, share_ref, sem):
    copies = [
        pltpu.make_async_copy(gradient_in, gradient_ref, sem.at[0]),
        pltpu.make_async_copy(share_in, share_ref, sem.at[1]),
        pltpu.make_async_copy(primal_in, primal_ref, sem.at[2]),
    ]
    for copy in copies:
        copy.start()
    for copy in copies:
        copy.wait()


def kernel(
    mem_count,
    job_count,
    cost_ref,
    coef_ref,
    member_ref,
    owner_ref,
    local_ref,
    duals_ref,
    capacity_ref,
    primal_ref,
    gradient_ref,
    share_ref,
    cost_v,
    coef_v,
    cost_w,
    coef_w,
    member_s,
    owner_s,
    local_s,
    owner_v,
    local_v,
    capacity_v,
    table,
    proxy,
    first_duals,
    list_v,
    list_s,
    match_v,
    column,
    totals,
    first_totals,
    incoming,
    member_part,
    member_in,
    load_sem,
    small_sem,
    list_sem,
    job_enter,
    proxy_send,
    proxy_recv,
    gather_send,
    gather_recv,
    column_send,
    column_recv,
    member_send,
    member_recv,
):
    slots, block = cost_v.shape[0], cost_v.shape[1]
    jobs = duals_ref.shape[0]
    my_mem = lax.axis_index("mem")
    my_job = lax.axis_index("job")
    is_head = my_mem == 0
    is_proxy = jnp.logical_and(my_mem > 0, my_mem <= PROXIES)
    mem_steps = range(1, mem_count)
    job_steps = range(1, job_count)

    barrier = pltpu.get_barrier_semaphore()

    def greet(*peer):
        pl.semaphore_signal(barrier, inc=1, device_id=peer, device_id_type=MESH)

    def flips(index, count):
        bits = range(count.bit_length() - 1)
        return [(1 << bit) - (2 << bit) * ((index // (1 << bit)) % 2) for bit in bits]

    mem_flips = flips(my_mem, mem_count)
    job_flips = flips(my_job, job_count)

    def mem_peer(distance):
        return my_mem + sum(flip for bit, flip in enumerate(mem_flips) if distance >> bit & 1)

    def job_peer(distance):
        return my_job + sum(flip for bit, flip in enumerate(job_flips) if distance >> bit & 1)

    other_job = job_peer(1)

    @pl.when(my_mem > PROXIES)
    def _():
        greet(PROXIES - my_mem % 2, other_job)

    @pl.when(is_proxy)
    def _():
        greet(0, other_job)

    own_duals = pltpu.make_async_copy(duals_ref, table.at[my_mem], small_sem.at[0])
    own_duals.start()
    for distance in mem_steps:
        peer = mem_peer(distance)

        @pl.when(peer > 0)
        def _():
            greet(peer, my_job)

    for distance in job_steps:
        peer = job_peer(distance)

        @pl.when(jnp.logical_or(my_mem <= PROXIES, peer > my_job))
        def _():
            greet(my_mem, peer)

    small = [
        own_duals,
        pltpu.make_async_copy(owner_ref, owner_s, small_sem.at[1]),
        pltpu.make_async_copy(local_ref, local_s, small_sem.at[2]),
        pltpu.make_async_copy(owner_ref, owner_v, small_sem.at[3]),
        pltpu.make_async_copy(local_ref, local_v, small_sem.at[4]),
        pltpu.make_async_copy(member_ref, member_s, small_sem.at[5]),
        pltpu.make_async_copy(capacity_ref, capacity_v, small_sem.at[6]),
    ]
    loads = [
        pltpu.make_async_copy(cost_ref, cost_v, load_sem.at[0]),
        pltpu.make_async_copy(coef_ref, coef_v, load_sem.at[1]),
    ]
    small[0].wait()

    def all_of(ref, count, send_sem, recv_sem):
        part = ref.at[pl.ds(0, count)]
        return pltpu.make_async_remote_copy(
            src_ref=part,
            dst_ref=part,
            send_sem=send_sem,
            recv_sem=recv_sem,
            device_id=(my_mem, other_job),
            device_id_type=MESH,
        )

    def to_proxy(mem):
        return pltpu.make_async_remote_copy(
            src_ref=table.at[0],
            dst_ref=proxy,
            send_sem=proxy_send.at[0],
            recv_sem=proxy_recv.at[0],
            device_id=(mem, other_job),
            device_id_type=MESH,
        )

    def from_proxy(mem):
        return pltpu.make_async_remote_copy(
            src_ref=proxy,
            dst_ref=table.at[0],
            send_sem=proxy_send.at[0],
            recv_sem=gather_recv.at[0],
            device_id=(mem, other_job),
            device_id_type=MESH,
        )

    def gather(distance, peer=None):
        peer = mem_peer(distance) if peer is None else peer
        return pltpu.make_async_remote_copy(
            src_ref=table.at[my_mem],
            dst_ref=table.at[my_mem],
            send_sem=gather_send.at[0],
            recv_sem=gather_recv.at[jnp.minimum(my_mem, FIRST)],
            device_id=(peer, my_job),
            device_id_type=MESH,
        )

    @pl.when(is_head)
    def _():
        pl.semaphore_wait(barrier, PROXIES + job_count - 1)
        for mem in range(1, PROXIES + 1):
            to_proxy(mem).start()

    @pl.when(my_mem > PROXIES)
    def _():
        pl.semaphore_wait(barrier, mem_count - 1 + my_job)
        gather(my_mem, 0).start()
        for distance in reversed(mem_steps):

            @pl.when(distance != my_mem)
            def _():
                gather(distance).start()

        for distance in job_steps:
            peer = job_peer(distance)

            @pl.when(peer < my_job)
            def _():
                pl.semaphore_signal(
                    job_enter,
                    inc=1,
                    device_id=(my_mem, peer),
                    device_id_type=MESH,
                )

    for copy in small[1:] + loads:
        copy.start()

    small[1].wait()
    small[2].wait()
    owners = lax.broadcasted_iota(jnp.int32, (8, block), 0)
    ranks = lax.broadcasted_iota(jnp.int32, (8, block), 1)

    def enlist(slot, carry):
        slot_list, local_list, count = carry
        hit = owners == owner_s[0, slot]
        put = jnp.logical_and(hit, ranks == count)
        return (
            jnp.where(put, slot, slot_list),
            jnp.where(put, local_s[0, slot], local_list),
            jnp.where(hit, count + 1, count),
        )

    zeros = jnp.zeros((8, block), jnp.int32)
    slot_list, local_list, _ = lax.fori_loop(
        0, slots, enlist, (zeros, zeros - 1, zeros), unroll=4
    )
    list_v[0] = slot_list
    list_v[1] = local_list
    listing = pltpu.make_async_copy(list_v, list_s, list_sem.at[0])
    listing.start()

    small[3].wait()
    small[4].wait()
    named = owner_v[...] * jobs + local_v[...]
    match = lax.broadcasted_iota(jnp.int32, (mem_count * jobs, slots), 0) == named
    match_v[...] = match.astype(jnp.float32).astype(jnp.bfloat16)

    for mine in range(1, PROXIES + 1):

        @pl.when(my_mem == mine)
        def _():
            served = range(mine, mem_count, PROXIES)
            pl.semaphore_wait(barrier, mem_count + job_count - 3 + len(served))
            to_proxy(mine).wait_recv()
            from_proxy(served[-1]).start()
            gather(mine, 0).start()
            others = [distance for distance in reversed(mem_steps) if distance != mine]
            for place, distance in enumerate(others):
                if place < len(served) - 1:
                    from_proxy(served[-2 - place]).start()
                gather(distance).start()

    for copy in small[5:]:
        copy.wait()
    for copy in loads:
        copy.wait()
    listing.wait()

    def widen(slot, carry):
        cost_w[slot] = cost_v[slot].astype(jnp.float32)
        coef_w[slot] = coef_v[slot].astype(jnp.float32)
        return carry

    lax.fori_loop(0, slots, widen, 0, unroll=2)

    rows_of_block = lax.broadcasted_iota(jnp.int32, (jobs, block), 0)

    def columns(source, distance, peer):
        return pltpu.make_async_remote_copy(
            src_ref=source,
            dst_ref=incoming.at[distance],
            send_sem=column_send.at[0],
            recv_sem=column_recv.at[0],
            device_id=(peer, my_job),
            device_id_type=MESH,
        )

    def columns_to(distance):
        peer = mem_peer(distance)
        rows = pl.ds(pl.multiple_of(peer * jobs, jobs), jobs)
        return columns(totals.at[rows], distance, peer)

    def allocate(slot, dual):
        return jnp.clip(coef_w[slot] * dual - cost_w[slot], 0.0, 1.0)

    def column_sums(slot, allocation):
        return jnp.sum(coef_w[slot] * allocation, axis=0, keepdims=True)

    for owner in range(FIRST):

        @pl.when(my_mem > owner)
        def _():
            distance = partner(my_mem, owner, mem_count)
            pltpu.make_async_remote_copy(
                src_ref=table.at[owner],
                dst_ref=table.at[owner],
                send_sem=gather_send.at[0],
                recv_sem=gather_recv.at[owner],
                device_id=(owner, my_job),
                device_id_type=MESH,
            ).wait_recv()
            first_duals[...] = -table[owner]
            total = jnp.zeros((jobs, block), jnp.float32)
            for rank in range(min(PEER_MOST, slots)):
                slot = list_s[0, owner, rank]
                local = list_s[1, owner, rank]
                dual = first_duals[pl.ds(jnp.maximum(local, 0), 1), :]
                sums = column_sums(slot, allocate(slot, dual))
                total = total + jnp.where(rows_of_block == local, sums, 0.0)
            first_totals[owner] = total
            columns(first_totals.at[owner], distance, owner).start()

    def later(distance):
        peer = mem_peer(distance)
        return peer >= jnp.minimum(my_mem, FIRST)

    for owner in range(1, FIRST):

        @pl.when(my_mem < owner)
        def _():
            all_of(table, 1, gather_send.at[0], gather_recv.at[owner]).wait_recv()

    @pl.when(my_mem < FIRST)
    def _():
        others = mem_count - FIRST
        all_of(table, others, gather_send.at[0], gather_recv.at[FIRST]).wait_recv()

    @pl.when(my_mem >= FIRST)
    def _():
        others = mem_count - FIRST - 1
        all_of(table, others, gather_send.at[0], gather_recv.at[FIRST]).wait_recv()

    member_rows = lax.broadcasted_iota(jnp.int32, (MB_DEV, block), 0)

    def allocate_all(keep):
        def group(index, members):
            parts, marks = [], []
            for side in range(GROUP):
                slot = GROUP * index + side
                dual = -table[owner_s[0, slot], pl.ds(local_s[0, slot], 1), :]
                allocation = allocate(slot, dual)
                part = allocation.astype(jnp.bfloat16)
                primal_ref[slot] = part
                keep(slot, allocation)
                mark = (member_rows == member_s[0, slot]).astype(jnp.float32)
                parts.append(part)
                marks.append(mark.astype(jnp.bfloat16))
            return members + lax.dot_general(
                jnp.concatenate(marks, axis=1),
                jnp.concatenate(parts, axis=1),
                (((1,), (1,)), ((), ())),
                preferred_element_type=jnp.float32,
            )

        member_part[...] = lax.fori_loop(
            0, slots // GROUP, group, jnp.zeros((MB_DEV, block), jnp.float32), unroll=True
        )

    def keep_sums(slot, allocation):
        column[pl.ds(slot, 1), :] = column_sums(slot, allocation)

    def keep_allocation(slot, allocation):
        cost_w[slot] = allocation

    def send_columns():
        match = match_v[...]
        sums = column[...]
        high = sums.astype(jnp.bfloat16)
        low = (sums - high.astype(jnp.float32)).astype(jnp.bfloat16)
        totals[...] = jnp.dot(match, high, preferred_element_type=jnp.float32) + jnp.dot(
            match, low, preferred_element_type=jnp.float32
        )
        for distance in reversed(mem_steps):

            @pl.when(later(distance))
            def _():
                columns_to(distance).start()

    def shares(distance):
        return pltpu.make_async_remote_copy(
            src_ref=member_part,
            dst_ref=member_in.at[distance],
            send_sem=member_send.at[0],
            recv_sem=member_recv.at[0],
            device_id=(my_mem, job_peer(distance)),
            device_id_type=MESH,
        )

    def send_shares():
        higher = job_count - 1 - my_job

        @pl.when(jnp.logical_and(my_mem > PROXIES, higher > 0))
        def _():
            pl.semaphore_wait(job_enter, higher)

        for distance in sorted(job_steps, key=lambda step: step % 2):
            shares(distance).start()

    @pl.when(is_head)
    def _():
        allocate_all(keep_allocation)
        send_shares()

        def sum_up(slot, carry):
            keep_sums(slot, cost_w[slot])
            return carry

        lax.fori_loop(0, slots, sum_up, 0, unroll=GROUP)
        send_columns()

    @pl.when(jnp.logical_not(is_head))
    def _():
        allocate_all(keep_sums)
        send_columns()
        send_shares()

    own_rows = pl.ds(pl.multiple_of(my_mem * jobs, jobs), jobs)
    gradient = totals[own_rows, :] - capacity_v[...].astype(jnp.float32)

    @pl.when(is_head)
    def _():
        all_of(table, PROXIES, proxy_send.at[0], proxy_recv.at[0]).wait_send()

    for mine in range(1, PROXIES + 1):

        @pl.when(my_mem == mine)
        def _():
            served = len(range(mine, mem_count, PROXIES))
            all_of(table, served, proxy_send.at[0], proxy_recv.at[0]).wait_send()

    @pl.when(jnp.logical_not(is_head))
    def _():
        all_of(table, mem_count - 1, gather_send.at[0], gather_recv.at[0]).wait_send()

    all_shares = all_of(member_in.at[pl.ds(1, job_count - 1)], job_count - 1, member_send.at[0], member_recv.at[0])
    all_shares.wait_recv()
    share = member_part[...]
    for distance in job_steps:
        share = share + member_in[distance]
    share_ref[...] = share * (1.0 / block)
    all_shares.wait_send()
    all_columns = all_of(incoming.at[pl.ds(1, mem_count - 1)], mem_count - 1, column_send.at[0], column_recv.at[0])
    all_columns.wait_send()
    all_columns.wait_recv()
    for distance in mem_steps:
        gradient = gradient + incoming[distance]
    gradient_ref[...] = gradient


def solution(mesh):
    mem_count, job_count = mesh.shape["mem"], mesh.shape["job"]
    row = P(("mem", "job"))

    def per_device(pair_cost, pair_coef, slot_member, slot_owner, slot_local, duals, capacity):
        slots, block, _ = pair_cost.shape
        jobs = duals.shape[0]
        hbm = pl.BlockSpec(memory_space=pltpu.HBM)
        vmem = pl.BlockSpec(memory_space=pltpu.VMEM)
        dma = pltpu.SemaphoreType.DMA
        out_shape = (
            jax.ShapeDtypeStruct(pair_cost.shape, jnp.bfloat16),
            jax.ShapeDtypeStruct((jobs, block), jnp.float32),
            jax.ShapeDtypeStruct((MB_DEV, block), jnp.float32),
        )
        operands = (
            pair_cost,
            pair_coef,
            slot_member,
            slot_owner.reshape(1, slots),
            slot_local,
            duals,
            capacity,
        )
        operands = [pltpu.with_memory_space_constraint(value, pltpu.HBM) for value in operands]
        results = pl.pallas_call(
            functools.partial(kernel, mem_count, job_count),
            out_shape=out_shape,
            in_specs=[hbm] * 7,
            out_specs=(vmem,) * 3,
            scratch_shapes=[
                pltpu.VMEM(pair_cost.shape, jnp.bfloat16),
                pltpu.VMEM(pair_cost.shape, jnp.bfloat16),
                pltpu.VMEM(pair_cost.shape, jnp.float32),
                pltpu.VMEM(pair_cost.shape, jnp.float32),
                pltpu.SMEM((1, slots), jnp.int32),
                pltpu.SMEM((1, slots), jnp.int32),
                pltpu.SMEM((1, slots), jnp.int32),
                pltpu.VMEM((1, slots), jnp.int32),
                pltpu.VMEM((1, slots), jnp.int32),
                pltpu.VMEM((jobs, block), jnp.int32),
                pltpu.VMEM((mem_count, jobs, block), jnp.float32),
                pltpu.VMEM((jobs, block), jnp.float32),
                pltpu.VMEM((jobs, block), jnp.float32),
                pltpu.VMEM((2, 8, block), jnp.int32),
                pltpu.SMEM((2, 8, block), jnp.int32),
                pltpu.VMEM((mem_count * jobs, slots), jnp.bfloat16),
                pltpu.VMEM((slots, block), jnp.float32),
                pltpu.VMEM((mem_count * jobs, block), jnp.float32),
                pltpu.VMEM((FIRST, jobs, block), jnp.float32),
                pltpu.VMEM((mem_count, jobs, block), jnp.float32),
                pltpu.VMEM((MB_DEV, block), jnp.float32),
                pltpu.VMEM((job_count, MB_DEV, block), jnp.float32),
                dma((2,)),
                dma((7,)),
                dma((1,)),
                pltpu.SemaphoreType.REGULAR,
                dma((1,)),
                dma((1,)),
                dma((1,)),
                dma((FIRST + 1,)),
                dma((1,)),
                dma((1,)),
                dma((1,)),
                dma((1,)),
            ],
            compiler_params=pltpu.CompilerParams(
                collective_id=0, has_side_effects=True, vmem_limit_bytes=VMEM_LIMIT
            ),
        )(*operands)
        return pl.pallas_call(
            finish,
            out_shape=out_shape,
            in_specs=[pl.BlockSpec(memory_space=pl.ANY)] * 3,
            out_specs=(hbm,) * 3,
            scratch_shapes=[dma((3,))],
            compiler_params=pltpu.CompilerParams(vmem_limit_bytes=VMEM_LIMIT),
        )(*results)

    return jax.shard_map(
        per_device,
        mesh=mesh,
        in_specs=(row,) * 7,
        out_specs=(row, row, P("mem")),
        check_vma=False,
    )
```

```python
import functools

import jax
import jax.numpy as jnp
from jax import lax
from jax.experimental import pallas as pl
from jax.experimental.pallas import tpu as pltpu
from jax.sharding import PartitionSpec as P

MB_DEV = 32
PEER_MOST = 9
FIRST = 2
PROXIES = 2
GROUP = 8
VMEM_LIMIT = 16 << 20

MESH = pl.DeviceIdType.MESH


def partner(index, distance, count):
    assert count & (count - 1) == 0
    bit = 1
    while bit < count:
        flip = (distance // bit) % 2
        index = index + flip * (bit - 2 * bit * ((index // bit) % 2))
        bit *= 2
    return index


def finish(primal_in, gradient_in, share_in, primal_ref, gradient_ref, share_ref, sem):
    copies = [
        pltpu.make_async_copy(gradient_in, gradient_ref, sem.at[0]),
        pltpu.make_async_copy(share_in, share_ref, sem.at[1]),
        pltpu.make_async_copy(primal_in, primal_ref, sem.at[2]),
    ]
    for copy in copies:
        copy.start()
    for copy in copies:
        copy.wait()


def kernel(
    mem_count,
    job_count,
    cost_ref,
    coef_ref,
    member_ref,
    owner_ref,
    local_ref,
    duals_ref,
    capacity_ref,
    primal_ref,
    gradient_ref,
    share_ref,
    cost_v,
    coef_v,
    cost_w,
    coef_w,
    member_s,
    owner_s,
    local_s,
    owner_v,
    local_v,
    capacity_v,
    table,
    proxy,
    first_duals,
    list_v,
    list_s,
    match_v,
    column,
    totals,
    first_totals,
    incoming,
    member_part,
    member_in,
    load_sem,
    small_sem,
    list_sem,
    job_enter,
    late_enter,
    proxy_send,
    proxy_recv,
    gather_send,
    gather_recv,
    column_send,
    column_recv,
    member_send,
    member_recv,
):
    slots, block = cost_v.shape[0], cost_v.shape[1]
    jobs = duals_ref.shape[0]
    my_mem = lax.axis_index("mem")
    my_job = lax.axis_index("job")
    is_head = my_mem == 0
    is_proxy = jnp.logical_and(my_mem > 0, my_mem <= PROXIES)
    mem_steps = range(1, mem_count)
    job_steps = range(1, job_count)

    barrier = pltpu.get_barrier_semaphore()

    def greet(*peer):
        pl.semaphore_signal(barrier, inc=1, device_id=peer, device_id_type=MESH)

    def flips(index, count):
        bits = range(count.bit_length() - 1)
        return [(1 << bit) - (2 << bit) * ((index // (1 << bit)) % 2) for bit in bits]

    mem_flips = flips(my_mem, mem_count)
    job_flips = flips(my_job, job_count)

    def mem_peer(distance):
        return my_mem + sum(flip for bit, flip in enumerate(mem_flips) if distance >> bit & 1)

    def job_peer(distance):
        return my_job + sum(flip for bit, flip in enumerate(job_flips) if distance >> bit & 1)

    other_job = job_peer(1)
    late = mem_count - mem_count // 4
    odd_job = my_job % 2 == 1
    answers = jnp.logical_and(odd_job, my_mem >= late)

    @pl.when(my_mem > PROXIES)
    def _():
        greet(PROXIES - my_mem % 2, other_job)

    @pl.when(is_proxy)
    def _():
        greet(0, other_job)

    own_duals = pltpu.make_async_copy(duals_ref, table.at[my_mem], small_sem.at[0])
    own_duals.start()
    for distance in mem_steps:
        peer = mem_peer(distance)

        by_own_signal = jnp.logical_and(peer == 1, answers)

        @pl.when(jnp.logical_and(peer > 0, jnp.logical_not(by_own_signal)))
        def _():
            greet(peer, my_job)

    for distance in job_steps:
        peer = job_peer(distance)

        @pl.when(jnp.logical_or(my_mem <= PROXIES, peer > my_job))
        def _():
            greet(my_mem, peer)

    small = [
        own_duals,
        pltpu.make_async_copy(owner_ref, owner_s, small_sem.at[1]),
        pltpu.make_async_copy(local_ref, local_s, small_sem.at[2]),
        pltpu.make_async_copy(owner_ref, owner_v, small_sem.at[3]),
        pltpu.make_async_copy(local_ref, local_v, small_sem.at[4]),
        pltpu.make_async_copy(member_ref, member_s, small_sem.at[5]),
        pltpu.make_async_copy(capacity_ref, capacity_v, small_sem.at[6]),
    ]
    loads = [
        pltpu.make_async_copy(cost_ref, cost_v, load_sem.at[0]),
        pltpu.make_async_copy(coef_ref, coef_v, load_sem.at[1]),
    ]
    small[0].wait()

    def all_of(ref, count, send_sem, recv_sem):
        part = ref.at[pl.ds(0, count)]
        return pltpu.make_async_remote_copy(
            src_ref=part,
            dst_ref=part,
            send_sem=send_sem,
            recv_sem=recv_sem,
            device_id=(my_mem, other_job),
            device_id_type=MESH,
        )

    def to_proxy(mem):
        return pltpu.make_async_remote_copy(
            src_ref=table.at[0],
            dst_ref=proxy,
            send_sem=proxy_send.at[0],
            recv_sem=proxy_recv.at[0],
            device_id=(mem, other_job),
            device_id_type=MESH,
        )

    def from_proxy(mem, rows=pl.ds(0, jobs)):
        return pltpu.make_async_remote_copy(
            src_ref=proxy.at[rows],
            dst_ref=table.at[0, rows],
            send_sem=proxy_send.at[0],
            recv_sem=gather_recv.at[0],
            device_id=(mem, other_job),
            device_id_type=MESH,
        )

    def gather(distance, peer=None):
        peer = mem_peer(distance) if peer is None else peer
        return pltpu.make_async_remote_copy(
            src_ref=table.at[my_mem],
            dst_ref=table.at[my_mem],
            send_sem=gather_send.at[0],
            recv_sem=gather_recv.at[jnp.minimum(my_mem, FIRST)],
            device_id=(peer, my_job),
            device_id_type=MESH,
        )

    @pl.when(is_head)
    def _():
        pl.semaphore_wait(barrier, PROXIES + job_count - 1)
        for mem in range(1, PROXIES + 1):
            to_proxy(mem).start()

    @pl.when(my_mem > PROXIES)
    def _():
        pl.semaphore_wait(barrier, mem_count - 1 + my_job)

        @pl.when(answers)
        def _():
            pl.semaphore_signal(
                late_enter, inc=1, device_id=(1, my_job), device_id_type=MESH
            )

        gather(my_mem, 0).start()
        for distance in reversed(mem_steps):

            @pl.when(distance != my_mem)
            def _():
                gather(distance).start()

        for distance in job_steps:
            peer = job_peer(distance)

            @pl.when(peer < my_job)
            def _():
                pl.semaphore_signal(
                    job_enter,
                    inc=1,
                    device_id=(my_mem, peer),
                    device_id_type=MESH,
                )

    for copy in small[1:] + loads:
        copy.start()

    small[1].wait()
    small[2].wait()
    owners = lax.broadcasted_iota(jnp.int32, (8, block), 0)
    ranks = lax.broadcasted_iota(jnp.int32, (8, block), 1)

    def enlist(slot, carry):
        slot_list, local_list, count = carry
        hit = owners == owner_s[0, slot]
        put = jnp.logical_and(hit, ranks == count)
        return (
            jnp.where(put, slot, slot_list),
            jnp.where(put, local_s[0, slot], local_list),
            jnp.where(hit, count + 1, count),
        )

    zeros = jnp.zeros((8, block), jnp.int32)
    slot_list, local_list, _ = lax.fori_loop(
        0, slots, enlist, (zeros, zeros - 1, zeros), unroll=4
    )
    list_v[0] = slot_list
    list_v[1] = local_list
    listing = pltpu.make_async_copy(list_v, list_s, list_sem.at[0])
    listing.start()

    small[3].wait()
    small[4].wait()
    named = owner_v[...] * jobs + local_v[...]
    match = lax.broadcasted_iota(jnp.int32, (mem_count * jobs, slots), 0) == named
    match_v[...] = match.astype(jnp.float32).astype(jnp.bfloat16)

    for mine in range(1, PROXIES + 1):

        @pl.when(my_mem == mine)
        def _():
            served = range(mine, mem_count, PROXIES)
            left_out = jnp.where(odd_job, mem_count - late, 0) if mine == 1 else 0
            pl.semaphore_wait(barrier, mem_count + job_count - 3 + len(served) - left_out)
            to_proxy(mine).wait_recv()
            for half in range(2):
                from_proxy(served[-1], pl.ds(half * (jobs // 2), jobs // 2)).start()
            gather(mine, 0).start()
            others = [distance for distance in reversed(mem_steps) if distance != mine]
            for place, distance in enumerate(others):
                if place < len(served) - 1:
                    from_proxy(served[-2 - place]).start()
                if mine == 1 and distance >= late:

                    @pl.when(jnp.logical_not(odd_job))
                    def _():
                        gather(distance).start()

                else:
                    gather(distance).start()

            if mine == 1:

                @pl.when(odd_job)
                def _():
                    pl.semaphore_wait(late_enter, mem_count - late)
                    for distance in reversed(range(late, mem_count)):
                        gather(distance).start()


    for copy in small[5:]:
        copy.wait()
    for copy in loads:
        copy.wait()
    listing.wait()

    def widen(slot, carry):
        cost_w[slot] = cost_v[slot].astype(jnp.float32)
        coef_w[slot] = coef_v[slot].astype(jnp.float32)
        return carry

    lax.fori_loop(0, slots, widen, 0, unroll=2)

    rows_of_block = lax.broadcasted_iota(jnp.int32, (jobs, block), 0)

    def columns(source, distance, peer, rows):
        return pltpu.make_async_remote_copy(
            src_ref=source.at[rows],
            dst_ref=incoming.at[distance, rows],
            send_sem=column_send.at[0],
            recv_sem=column_recv.at[0],
            device_id=(peer, my_job),
            device_id_type=MESH,
        )

    def columns_to(distance):
        peer = mem_peer(distance)
        rows = pl.ds(pl.multiple_of(peer * jobs, jobs), jobs)
        return columns(totals.at[rows], distance, peer, pl.ds(0, jobs))

    def allocate(slot, dual):
        return jnp.clip(coef_w[slot] * dual - cost_w[slot], 0.0, 1.0)

    def column_sums(slot, allocation):
        return jnp.sum(coef_w[slot] * allocation, axis=0, keepdims=True)

    for owner in range(FIRST):

        @pl.when(my_mem > owner)
        def _():
            distance = partner(my_mem, owner, mem_count)
            pltpu.make_async_remote_copy(
                src_ref=table.at[owner],
                dst_ref=table.at[owner],
                send_sem=gather_send.at[0],
                recv_sem=gather_recv.at[owner],
                device_id=(owner, my_job),
                device_id_type=MESH,
            ).wait_recv()
            first_duals[...] = -table[owner]
            total = jnp.zeros((jobs, block), jnp.float32)
            for rank in range(min(PEER_MOST, slots)):
                slot = list_s[0, owner, rank]
                local = list_s[1, owner, rank]
                dual = first_duals[pl.ds(jnp.maximum(local, 0), 1), :]
                sums = column_sums(slot, allocate(slot, dual))
                total = total + jnp.where(rows_of_block == local, sums, 0.0)
            first_totals[owner] = total
            for half in range(2):
                rows = pl.ds(half * (jobs // 2), jobs // 2)
                columns(first_totals.at[owner], distance, owner, rows).start()

    def later(distance):
        peer = mem_peer(distance)
        return peer >= jnp.minimum(my_mem, FIRST)

    for owner in range(1, FIRST):

        @pl.when(my_mem < owner)
        def _():
            all_of(table, 1, gather_send.at[0], gather_recv.at[owner]).wait_recv()

    @pl.when(my_mem < FIRST)
    def _():
        others = mem_count - FIRST
        all_of(table, others, gather_send.at[0], gather_recv.at[FIRST]).wait_recv()

    @pl.when(my_mem >= FIRST)
    def _():
        others = mem_count - FIRST - 1
        all_of(table, others, gather_send.at[0], gather_recv.at[FIRST]).wait_recv()

    member_rows = lax.broadcasted_iota(jnp.int32, (MB_DEV, block), 0)

    def allocate_all(keep):
        def group(index, members):
            parts, marks = [], []
            for side in range(GROUP):
                slot = GROUP * index + side
                dual = -table[owner_s[0, slot], pl.ds(local_s[0, slot], 1), :]
                allocation = allocate(slot, dual)
                part = allocation.astype(jnp.bfloat16)
                primal_ref[slot] = part
                keep(slot, allocation)
                mark = (member_rows == member_s[0, slot]).astype(jnp.float32)
                parts.append(part)
                marks.append(mark.astype(jnp.bfloat16))
            return members + lax.dot_general(
                jnp.concatenate(marks, axis=1),
                jnp.concatenate(parts, axis=1),
                (((1,), (1,)), ((), ())),
                preferred_element_type=jnp.float32,
            )

        member_part[...] = lax.fori_loop(
            0, slots // GROUP, group, jnp.zeros((MB_DEV, block), jnp.float32), unroll=True
        )

    def keep_sums(slot, allocation):
        column[pl.ds(slot, 1), :] = column_sums(slot, allocation)

    def keep_allocation(slot, allocation):
        cost_w[slot] = allocation

    def send_columns():
        match = match_v[...]
        sums = column[...]
        high = sums.astype(jnp.bfloat16)
        low = (sums - high.astype(jnp.float32)).astype(jnp.bfloat16)
        totals[...] = jnp.dot(match, high, preferred_element_type=jnp.float32) + jnp.dot(
            match, low, preferred_element_type=jnp.float32
        )
        for distance in reversed(mem_steps):

            @pl.when(later(distance))
            def _():
                columns_to(distance).start()

    def shares(distance):
        return pltpu.make_async_remote_copy(
            src_ref=member_part,
            dst_ref=member_in.at[distance],
            send_sem=member_send.at[0],
            recv_sem=member_recv.at[0],
            device_id=(my_mem, job_peer(distance)),
            device_id_type=MESH,
        )

    def send_shares():
        higher = job_count - 1 - my_job

        @pl.when(jnp.logical_and(my_mem > PROXIES, higher > 0))
        def _():
            pl.semaphore_wait(job_enter, higher)

        for distance in sorted(job_steps, key=lambda step: step % 2):
            shares(distance).start()

    @pl.when(is_head)
    def _():
        allocate_all(keep_allocation)
        send_shares()

        def sum_up(slot, carry):
            keep_sums(slot, cost_w[slot])
            return carry

        lax.fori_loop(0, slots, sum_up, 0, unroll=GROUP)
        send_columns()

    @pl.when(jnp.logical_not(is_head))
    def _():
        allocate_all(keep_sums)
        send_columns()
        send_shares()

    own_rows = pl.ds(pl.multiple_of(my_mem * jobs, jobs), jobs)
    gradient = totals[own_rows, :] - capacity_v[...].astype(jnp.float32)

    @pl.when(is_head)
    def _():
        all_of(table, PROXIES, proxy_send.at[0], proxy_recv.at[0]).wait_send()

    for mine in range(1, PROXIES + 1):

        @pl.when(my_mem == mine)
        def _():
            served = len(range(mine, mem_count, PROXIES))
            all_of(table, served, proxy_send.at[0], proxy_recv.at[0]).wait_send()

    @pl.when(jnp.logical_not(is_head))
    def _():
        all_of(table, mem_count - 1, gather_send.at[0], gather_recv.at[0]).wait_send()

    all_shares = all_of(member_in.at[pl.ds(1, job_count - 1)], job_count - 1, member_send.at[0], member_recv.at[0])
    all_shares.wait_recv()
    share = member_part[...]
    for distance in job_steps:
        share = share + member_in[distance]
    share_ref[...] = share * (1.0 / block)
    all_shares.wait_send()
    all_columns = all_of(incoming.at[pl.ds(1, mem_count - 1)], mem_count - 1, column_send.at[0], column_recv.at[0])
    all_columns.wait_send()
    all_columns.wait_recv()
    for distance in mem_steps:
        gradient = gradient + incoming[distance]
    gradient_ref[...] = gradient


def solution(mesh):
    mem_count, job_count = mesh.shape["mem"], mesh.shape["job"]
    row = P(("mem", "job"))

    def per_device(pair_cost, pair_coef, slot_member, slot_owner, slot_local, duals, capacity):
        slots, block, _ = pair_cost.shape
        jobs = duals.shape[0]
        hbm = pl.BlockSpec(memory_space=pltpu.HBM)
        vmem = pl.BlockSpec(memory_space=pltpu.VMEM)
        dma = pltpu.SemaphoreType.DMA
        out_shape = (
            jax.ShapeDtypeStruct(pair_cost.shape, jnp.bfloat16),
            jax.ShapeDtypeStruct((jobs, block), jnp.float32),
            jax.ShapeDtypeStruct((MB_DEV, block), jnp.float32),
        )
        operands = (
            pair_cost,
            pair_coef,
            slot_member,
            slot_owner.reshape(1, slots),
            slot_local,
            duals,
            capacity,
        )
        operands = [pltpu.with_memory_space_constraint(value, pltpu.HBM) for value in operands]
        results = pl.pallas_call(
            functools.partial(kernel, mem_count, job_count),
            out_shape=out_shape,
            in_specs=[hbm] * 7,
            out_specs=(vmem,) * 3,
            scratch_shapes=[
                pltpu.VMEM(pair_cost.shape, jnp.bfloat16),
                pltpu.VMEM(pair_cost.shape, jnp.bfloat16),
                pltpu.VMEM(pair_cost.shape, jnp.float32),
                pltpu.VMEM(pair_cost.shape, jnp.float32),
                pltpu.SMEM((1, slots), jnp.int32),
                pltpu.SMEM((1, slots), jnp.int32),
                pltpu.SMEM((1, slots), jnp.int32),
                pltpu.VMEM((1, slots), jnp.int32),
                pltpu.VMEM((1, slots), jnp.int32),
                pltpu.VMEM((jobs, block), jnp.int32),
                pltpu.VMEM((mem_count, jobs, block), jnp.float32),
                pltpu.VMEM((jobs, block), jnp.float32),
                pltpu.VMEM((jobs, block), jnp.float32),
                pltpu.VMEM((2, 8, block), jnp.int32),
                pltpu.SMEM((2, 8, block), jnp.int32),
                pltpu.VMEM((mem_count * jobs, slots), jnp.bfloat16),
                pltpu.VMEM((slots, block), jnp.float32),
                pltpu.VMEM((mem_count * jobs, block), jnp.float32),
                pltpu.VMEM((FIRST, jobs, block), jnp.float32),
                pltpu.VMEM((mem_count, jobs, block), jnp.float32),
                pltpu.VMEM((MB_DEV, block), jnp.float32),
                pltpu.VMEM((job_count, MB_DEV, block), jnp.float32),
                dma((2,)),
                dma((7,)),
                dma((1,)),
                pltpu.SemaphoreType.REGULAR,
                pltpu.SemaphoreType.REGULAR,
                dma((1,)),
                dma((1,)),
                dma((1,)),
                dma((FIRST + 1,)),
                dma((1,)),
                dma((1,)),
                dma((1,)),
                dma((1,)),
            ],
            compiler_params=pltpu.CompilerParams(
                collective_id=0, has_side_effects=True, vmem_limit_bytes=VMEM_LIMIT
            ),
        )(*operands)
        return pl.pallas_call(
            finish,
            out_shape=out_shape,
            in_specs=[pl.BlockSpec(memory_space=pl.ANY)] * 3,
            out_specs=(hbm,) * 3,
            scratch_shapes=[dma((3,))],
            compiler_params=pltpu.CompilerParams(vmem_limit_bytes=VMEM_LIMIT),
        )(*results)

    return jax.shard_map(
        per_device,
        mesh=mesh,
        in_specs=(row,) * 7,
        out_specs=(row, row, P("mem")),
        check_vma=False,
    )
```

```python
import functools

import jax
import jax.numpy as jnp
from jax import lax
from jax.experimental import pallas as pl
from jax.experimental.pallas import tpu as pltpu
from jax.sharding import PartitionSpec as P

MB_DEV = 32
PEER_MOST = 9
FIRST = 2
PROXIES = 2
GROUP = 8
VMEM_LIMIT = 16 << 20

MESH = pl.DeviceIdType.MESH


def partner(index, distance, count):
    assert count & (count - 1) == 0
    bit = 1
    while bit < count:
        flip = (distance // bit) % 2
        index = index + flip * (bit - 2 * bit * ((index // bit) % 2))
        bit *= 2
    return index


def finish(primal_in, gradient_in, share_in, primal_ref, gradient_ref, share_ref, sem):
    copies = [
        pltpu.make_async_copy(gradient_in, gradient_ref, sem.at[0]),
        pltpu.make_async_copy(share_in, share_ref, sem.at[1]),
        pltpu.make_async_copy(primal_in, primal_ref, sem.at[2]),
    ]
    for copy in copies:
        copy.start()
    for copy in copies:
        copy.wait()


def kernel(
    mem_count,
    job_count,
    cost_ref,
    coef_ref,
    member_ref,
    owner_ref,
    local_ref,
    duals_ref,
    capacity_ref,
    primal_ref,
    gradient_ref,
    share_ref,
    pairs_v,
    cost_w,
    coef_w,
    member_s,
    owner_s,
    local_s,
    named_v,
    capacity_v,
    table,
    proxy,
    first_duals,
    list_v,
    list_s,
    match_v,
    column,
    totals,
    first_totals,
    incoming,
    member_part,
    member_in,
    load_sem,
    small_sem,
    list_sem,
    job_enter,
    late_enter,
    proxy_send,
    proxy_recv,
    gather_send,
    gather_recv,
    column_send,
    column_recv,
    member_send,
    member_recv,
):
    slots, block = cost_w.shape[0], cost_w.shape[1]
    jobs = duals_ref.shape[0]
    my_mem = lax.axis_index("mem")
    my_job = lax.axis_index("job")
    is_head = my_mem == 0
    is_proxy = jnp.logical_and(my_mem > 0, my_mem <= PROXIES)
    mem_steps = range(1, mem_count)
    job_steps = range(1, job_count)

    barrier = pltpu.get_barrier_semaphore()

    def greet(*peer):
        pl.semaphore_signal(barrier, inc=1, device_id=peer, device_id_type=MESH)

    def flips(index, count):
        bits = range(count.bit_length() - 1)
        return [(1 << bit) - (2 << bit) * ((index // (1 << bit)) % 2) for bit in bits]

    mem_flips = flips(my_mem, mem_count)
    job_flips = flips(my_job, job_count)

    def mem_peer(distance):
        return my_mem + sum(flip for bit, flip in enumerate(mem_flips) if distance >> bit & 1)

    def job_peer(distance):
        return my_job + sum(flip for bit, flip in enumerate(job_flips) if distance >> bit & 1)

    other_job = job_peer(1)
    late = mem_count - mem_count // 4
    odd_job = my_job % 2 == 1
    answers = jnp.logical_and(odd_job, my_mem >= late)

    @pl.when(my_mem > PROXIES)
    def _():
        greet(PROXIES - my_mem % 2, other_job)

    @pl.when(is_proxy)
    def _():
        greet(0, other_job)

    own_duals = pltpu.make_async_copy(duals_ref, table.at[my_mem], small_sem.at[0])
    own_duals.start()
    for distance in mem_steps:
        peer = mem_peer(distance)

        by_own_signal = jnp.logical_and(peer == 1, answers)

        @pl.when(jnp.logical_and(peer > 0, jnp.logical_not(by_own_signal)))
        def _():
            greet(peer, my_job)

    for distance in job_steps:
        peer = job_peer(distance)

        @pl.when(jnp.logical_or(my_mem <= PROXIES, peer > my_job))
        def _():
            greet(my_mem, peer)

    small = [
        own_duals,
        pltpu.make_async_copy(owner_ref, owner_s, small_sem.at[1]),
        pltpu.make_async_copy(local_ref, local_s, small_sem.at[2]),
        pltpu.make_async_copy(member_ref, member_s, small_sem.at[3]),
        pltpu.make_async_copy(capacity_ref, capacity_v, small_sem.at[4]),
    ]
    loads = [
        pltpu.make_async_copy(cost_ref, pairs_v.at[0], load_sem.at[0]),
        pltpu.make_async_copy(coef_ref, pairs_v.at[1], load_sem.at[0]),
    ]
    small[0].wait()

    def all_of(ref, count, send_sem, recv_sem):
        part = ref.at[pl.ds(0, count)]
        return pltpu.make_async_remote_copy(
            src_ref=part,
            dst_ref=part,
            send_sem=send_sem,
            recv_sem=recv_sem,
            device_id=(my_mem, other_job),
            device_id_type=MESH,
        )

    def to_proxy(mem):
        return pltpu.make_async_remote_copy(
            src_ref=table.at[0],
            dst_ref=proxy,
            send_sem=proxy_send.at[0],
            recv_sem=proxy_recv.at[0],
            device_id=(mem, other_job),
            device_id_type=MESH,
        )

    def from_proxy(mem, rows=pl.ds(0, jobs)):
        return pltpu.make_async_remote_copy(
            src_ref=proxy.at[rows],
            dst_ref=table.at[0, rows],
            send_sem=proxy_send.at[0],
            recv_sem=gather_recv.at[0],
            device_id=(mem, other_job),
            device_id_type=MESH,
        )

    def gather(distance, peer=None):
        peer = mem_peer(distance) if peer is None else peer
        return pltpu.make_async_remote_copy(
            src_ref=table.at[my_mem],
            dst_ref=table.at[my_mem],
            send_sem=gather_send.at[0],
            recv_sem=gather_recv.at[jnp.minimum(my_mem, FIRST)],
            device_id=(peer, my_job),
            device_id_type=MESH,
        )

    @pl.when(is_head)
    def _():
        pl.semaphore_wait(barrier, PROXIES + job_count - 1)
        for mem in range(1, PROXIES + 1):
            to_proxy(mem).start()

    @pl.when(my_mem > PROXIES)
    def _():
        pl.semaphore_wait(barrier, mem_count - 1 + my_job)

        @pl.when(answers)
        def _():
            pl.semaphore_signal(
                late_enter, inc=1, device_id=(1, my_job), device_id_type=MESH
            )

        gather(my_mem, 0).start()
        for distance in reversed(mem_steps):

            @pl.when(distance != my_mem)
            def _():
                gather(distance).start()

        for distance in job_steps:
            peer = job_peer(distance)

            @pl.when(peer < my_job)
            def _():
                pl.semaphore_signal(
                    job_enter,
                    inc=1,
                    device_id=(my_mem, peer),
                    device_id_type=MESH,
                )

    for copy in small[1:] + loads:
        copy.start()

    small[1].wait()
    small[2].wait()
    owners = lax.broadcasted_iota(jnp.int32, (8, block), 0)
    ranks = lax.broadcasted_iota(jnp.int32, (8, block), 1)

    def enlist(slot, carry):
        slot_list, local_list, count, named = carry
        row = owner_s[0, slot] * jobs + local_s[0, slot]
        hit = owners == owner_s[0, slot]
        put = jnp.logical_and(hit, ranks == count)
        return (
            jnp.where(put, slot, slot_list),
            jnp.where(put, local_s[0, slot], local_list),
            jnp.where(hit, count + 1, count),
            jnp.where(ranks == slot, row, named),
        )

    zeros = jnp.zeros((8, block), jnp.int32)
    slot_list, local_list, _, named = lax.fori_loop(
        0, slots, enlist, (zeros, zeros - 1, zeros, zeros), unroll=4
    )
    list_v[0] = slot_list
    list_v[1] = local_list
    listing = pltpu.make_async_copy(list_v, list_s, list_sem.at[0])
    listing.start()

    named_v[...] = named
    named = named_v[pl.ds(0, 1), pl.ds(0, slots)]
    match = lax.broadcasted_iota(jnp.int32, (mem_count * jobs, slots), 0) == named
    match_v[...] = match.astype(jnp.float32).astype(jnp.bfloat16)

    for mine in range(1, PROXIES + 1):

        @pl.when(my_mem == mine)
        def _():
            served = range(mine, mem_count, PROXIES)
            left_out = jnp.where(odd_job, mem_count - late, 0) if mine == 1 else 0
            to_proxy(mine).wait_recv()
            pl.semaphore_wait(barrier, mem_count + job_count - 3 + len(served) - left_out)
            for half in range(2):
                from_proxy(served[-1], pl.ds(half * (jobs // 2), jobs // 2)).start()
            gather(mine, 0).start()
            others = [distance for distance in reversed(mem_steps) if distance != mine]
            for place, distance in enumerate(others):
                if place < len(served) - 1:
                    from_proxy(served[-2 - place]).start()
                if mine == 1 and distance >= late:

                    @pl.when(jnp.logical_not(odd_job))
                    def _():
                        gather(distance).start()

                else:
                    gather(distance).start()

            if mine == 1:

                @pl.when(odd_job)
                def _():
                    pl.semaphore_wait(late_enter, mem_count - late)
                    for distance in reversed(range(late, mem_count)):
                        gather(distance).start()


    for copy in small[3:]:
        copy.wait()
    pltpu.make_async_copy(pairs_v, pairs_v, load_sem.at[0]).wait()
    listing.wait()

    def widen(slot, carry):
        cost_w[slot] = pairs_v[0, slot].astype(jnp.float32)
        coef_w[slot] = pairs_v[1, slot].astype(jnp.float32)
        return carry

    lax.fori_loop(0, slots, widen, 0, unroll=2)

    rows_of_block = lax.broadcasted_iota(jnp.int32, (jobs, block), 0)

    def columns(source, distance, peer, rows):
        return pltpu.make_async_remote_copy(
            src_ref=source.at[rows],
            dst_ref=incoming.at[distance, rows],
            send_sem=column_send.at[0],
            recv_sem=column_recv.at[0],
            device_id=(peer, my_job),
            device_id_type=MESH,
        )

    def columns_to(distance):
        peer = mem_peer(distance)
        rows = pl.ds(pl.multiple_of(peer * jobs, jobs), jobs)
        return columns(totals.at[rows], distance, peer, pl.ds(0, jobs))

    def allocate(slot, dual):
        return jnp.clip(coef_w[slot] * dual - cost_w[slot], 0.0, 1.0)

    def column_sums(slot, allocation):
        return jnp.sum(coef_w[slot] * allocation, axis=0, keepdims=True)

    for owner in range(FIRST):

        @pl.when(my_mem > owner)
        def _():
            distance = partner(my_mem, owner, mem_count)
            pltpu.make_async_remote_copy(
                src_ref=table.at[owner],
                dst_ref=table.at[owner],
                send_sem=gather_send.at[0],
                recv_sem=gather_recv.at[owner],
                device_id=(owner, my_job),
                device_id_type=MESH,
            ).wait_recv()
            first_duals[...] = -table[owner]
            total = jnp.zeros((jobs, block), jnp.float32)
            for rank in range(min(PEER_MOST, slots)):
                slot = list_s[0, owner, rank]
                local = list_s[1, owner, rank]
                dual = first_duals[pl.ds(jnp.maximum(local, 0), 1), :]
                sums = column_sums(slot, allocate(slot, dual))
                total = total + jnp.where(rows_of_block == local, sums, 0.0)
            first_totals[owner] = total
            for half in range(2):
                rows = pl.ds(half * (jobs // 2), jobs // 2)
                columns(first_totals.at[owner], distance, owner, rows).start()

    def later(distance):
        peer = mem_peer(distance)
        return peer >= jnp.minimum(my_mem, FIRST)

    for owner in range(1, FIRST):

        @pl.when(my_mem < owner)
        def _():
            all_of(table, 1, gather_send.at[0], gather_recv.at[owner]).wait_recv()

    @pl.when(my_mem < FIRST)
    def _():
        others = mem_count - FIRST
        all_of(table, others, gather_send.at[0], gather_recv.at[FIRST]).wait_recv()

    @pl.when(my_mem >= FIRST)
    def _():
        others = mem_count - FIRST - 1
        all_of(table, others, gather_send.at[0], gather_recv.at[FIRST]).wait_recv()

    member_rows = lax.broadcasted_iota(jnp.int32, (MB_DEV, block), 0)

    def allocate_all(keep):
        def group(index, members):
            parts, marks = [], []
            for side in range(GROUP):
                slot = GROUP * index + side
                dual = -table[owner_s[0, slot], pl.ds(local_s[0, slot], 1), :]
                allocation = allocate(slot, dual)
                part = allocation.astype(jnp.bfloat16)
                primal_ref[slot] = part
                keep(slot, allocation)
                mark = (member_rows == member_s[0, slot]).astype(jnp.float32)
                parts.append(part)
                marks.append(mark.astype(jnp.bfloat16))
            return members + lax.dot_general(
                jnp.concatenate(marks, axis=1),
                jnp.concatenate(parts, axis=1),
                (((1,), (1,)), ((), ())),
                preferred_element_type=jnp.float32,
            )

        member_part[...] = lax.fori_loop(
            0, slots // GROUP, group, jnp.zeros((MB_DEV, block), jnp.float32), unroll=True
        )

    def keep_sums(slot, allocation):
        column[pl.ds(slot, 1), :] = column_sums(slot, allocation)

    def keep_allocation(slot, allocation):
        cost_w[slot] = allocation

    def send_columns():
        match = match_v[...]
        sums = column[...]
        high = sums.astype(jnp.bfloat16)
        low = (sums - high.astype(jnp.float32)).astype(jnp.bfloat16)
        totals[...] = jnp.dot(match, high, preferred_element_type=jnp.float32) + jnp.dot(
            match, low, preferred_element_type=jnp.float32
        )
        for distance in reversed(mem_steps):

            @pl.when(later(distance))
            def _():
                columns_to(distance).start()

    def shares(distance):
        return pltpu.make_async_remote_copy(
            src_ref=member_part,
            dst_ref=member_in.at[distance],
            send_sem=member_send.at[0],
            recv_sem=member_recv.at[0],
            device_id=(my_mem, job_peer(distance)),
            device_id_type=MESH,
        )

    def send_shares():
        higher = job_count - 1 - my_job

        @pl.when(jnp.logical_and(my_mem > PROXIES, higher > 0))
        def _():
            pl.semaphore_wait(job_enter, higher)

        for distance in sorted(job_steps, key=lambda step: step % 2):
            shares(distance).start()

    @pl.when(is_head)
    def _():
        allocate_all(keep_allocation)
        send_shares()

        def sum_up(slot, carry):
            keep_sums(slot, cost_w[slot])
            return carry

        lax.fori_loop(0, slots, sum_up, 0, unroll=GROUP)
        send_columns()

    @pl.when(jnp.logical_not(is_head))
    def _():
        allocate_all(keep_sums)
        send_columns()
        send_shares()

    own_rows = pl.ds(pl.multiple_of(my_mem * jobs, jobs), jobs)
    gradient = totals[own_rows, :] - capacity_v[...].astype(jnp.float32)

    @pl.when(is_head)
    def _():
        all_of(table, PROXIES, proxy_send.at[0], proxy_recv.at[0]).wait_send()

    for mine in range(1, PROXIES + 1):

        @pl.when(my_mem == mine)
        def _():
            served = len(range(mine, mem_count, PROXIES))
            all_of(table, served, proxy_send.at[0], proxy_recv.at[0]).wait_send()

    @pl.when(jnp.logical_not(is_head))
    def _():
        all_of(table, mem_count - 1, gather_send.at[0], gather_recv.at[0]).wait_send()

    all_shares = all_of(member_in.at[pl.ds(1, job_count - 1)], job_count - 1, member_send.at[0], member_recv.at[0])
    all_shares.wait_recv()
    share = member_part[...]
    for distance in job_steps:
        share = share + member_in[distance]
    share_ref[...] = share * (1.0 / block)
    all_shares.wait_send()
    all_columns = all_of(incoming.at[pl.ds(1, mem_count - 1)], mem_count - 1, column_send.at[0], column_recv.at[0])
    all_columns.wait_send()
    all_columns.wait_recv()
    for distance in mem_steps:
        gradient = gradient + incoming[distance]
    gradient_ref[...] = gradient


def solution(mesh):
    mem_count, job_count = mesh.shape["mem"], mesh.shape["job"]
    row = P(("mem", "job"))

    def per_device(pair_cost, pair_coef, slot_member, slot_owner, slot_local, duals, capacity):
        slots, block, _ = pair_cost.shape
        jobs = duals.shape[0]
        hbm = pl.BlockSpec(memory_space=pltpu.HBM)
        vmem = pl.BlockSpec(memory_space=pltpu.VMEM)
        dma = pltpu.SemaphoreType.DMA
        out_shape = (
            jax.ShapeDtypeStruct(pair_cost.shape, jnp.bfloat16),
            jax.ShapeDtypeStruct((jobs, block), jnp.float32),
            jax.ShapeDtypeStruct((MB_DEV, block), jnp.float32),
        )
        operands = (
            pair_cost,
            pair_coef,
            slot_member,
            slot_owner.reshape(1, slots),
            slot_local,
            duals,
            capacity,
        )
        operands = [pltpu.with_memory_space_constraint(value, pltpu.HBM) for value in operands]
        results = pl.pallas_call(
            functools.partial(kernel, mem_count, job_count),
            out_shape=out_shape,
            in_specs=[hbm] * 7,
            out_specs=(vmem,) * 3,
            scratch_shapes=[
                pltpu.VMEM((2, *pair_cost.shape), jnp.bfloat16),
                pltpu.VMEM(pair_cost.shape, jnp.float32),
                pltpu.VMEM(pair_cost.shape, jnp.float32),
                pltpu.SMEM((1, slots), jnp.int32),
                pltpu.SMEM((1, slots), jnp.int32),
                pltpu.SMEM((1, slots), jnp.int32),
                pltpu.VMEM((8, block), jnp.int32),
                pltpu.VMEM((jobs, block), jnp.int32),
                pltpu.VMEM((mem_count, jobs, block), jnp.float32),
                pltpu.VMEM((jobs, block), jnp.float32),
                pltpu.VMEM((jobs, block), jnp.float32),
                pltpu.VMEM((2, 8, block), jnp.int32),
                pltpu.SMEM((2, 8, block), jnp.int32),
                pltpu.VMEM((mem_count * jobs, slots), jnp.bfloat16),
                pltpu.VMEM((slots, block), jnp.float32),
                pltpu.VMEM((mem_count * jobs, block), jnp.float32),
                pltpu.VMEM((FIRST, jobs, block), jnp.float32),
                pltpu.VMEM((mem_count, jobs, block), jnp.float32),
                pltpu.VMEM((MB_DEV, block), jnp.float32),
                pltpu.VMEM((job_count, MB_DEV, block), jnp.float32),
                dma((1,)),
                dma((5,)),
                dma((1,)),
                pltpu.SemaphoreType.REGULAR,
                pltpu.SemaphoreType.REGULAR,
                dma((1,)),
                dma((1,)),
                dma((1,)),
                dma((FIRST + 1,)),
                dma((1,)),
                dma((1,)),
                dma((1,)),
                dma((1,)),
            ],
            compiler_params=pltpu.CompilerParams(
                collective_id=0, has_side_effects=True, vmem_limit_bytes=VMEM_LIMIT
            ),
        )(*operands)
        return pl.pallas_call(
            finish,
            out_shape=out_shape,
            in_specs=[pl.BlockSpec(memory_space=pl.ANY)] * 3,
            out_specs=(hbm,) * 3,
            scratch_shapes=[dma((3,))],
            compiler_params=pltpu.CompilerParams(vmem_limit_bytes=VMEM_LIMIT),
        )(*results)

    return jax.shard_map(
        per_device,
        mesh=mesh,
        in_specs=(row,) * 7,
        out_specs=(row, row, P("mem")),
        check_vma=False,
    )
```
